256 devices in a mesh: dp: 8 (over y_lo, x), lon: 32 (over y_hi, z, core).
Axes of the slice: x: 4, y: 4 (y_hi: 2, y_lo: 2; y = y_hi * 2 + y_lo), z: 8, core: 2. Of those that a mesh axis runs over, the one named last changes fastest.
Arguments:
- fields: bfloat16 [8, 64, 512, 384], P('dp', None, 'lon'), may hold values from -6 to 6
- cotangent: bfloat16 [8, 64, 512, 384], P('dp', None, 'lon'), may hold values from -6 to 6
- kernel_first: bfloat16 [3, 3, 64, 64], replicated, may hold values from -0.25 to 0.25
- kernel_second: bfloat16 [3, 3, 64, 64], replicated, may hold values from -0.25 to 0.25
- metric: float32 [384], replicated, may hold values from 0.5 to 3
Outputs:
- field_grad: bfloat16 [8, 64, 512, 384], P('dp', None, 'lon')
- grad_first: bfloat16 [3, 3, 64, 64], replicated
- grad_second: bfloat16 [3, 3, 64, 64], replicated
The draws below stay inside these ranges and needn't reach their ends.
All inputs are finite; a program needn't handle non-finite values.
Results may differ from the reference program's by a relative error of at most 0.0063.
Values may be sent and summed in bfloat16 or wider, within the bound.
A program may use at most 64 MiB of HBM per device.

```python
import math
import jax
import jax.numpy as jnp
from jax import lax

C = 64
LAT = 384
LON = 512
SAMPLES = 8


def levels(own_key, dims, cuts, least, largest):
    loudness = 1.0
    for position, blocks in cuts:
        draws = jax.random.uniform(jax.random.fold_in(jax.random.fold_in(own_key, 6), position), (blocks,), jnp.float32, least / len(cuts), largest / len(cuts))
        loudness = loudness * jnp.repeat(jnp.exp(draws), dims[position] // blocks).reshape((-1,) + (1,) * (len(dims) - 1 - position))
    return loudness


def scatter_about(key, shape, deviation, most, split=(), kind=jnp.bfloat16):
    loudness = levels(key, shape, split, -0.22, 0.18) if split else 1.0
    array = jax.random.normal(key, shape, jnp.float32) * deviation * loudness
    return jnp.minimum(jnp.maximum(array, -most), most).astype(kind)


def setup_inputs(seed: int = 0) -> dict:
    key_list = jax.random.split(jax.random.key(seed), 6)
    fields = scatter_about(key_list[0], (SAMPLES, C, LON, LAT), 1.0, 6.0, ((0, 8), (2, 32)))
    cotangent = scatter_about(key_list[1], (SAMPLES, C, LON, LAT), 1.0, 6.0, ((0, 8), (2, 32)))
    kernel_first = scatter_about(key_list[2], (3, 3, C, C), (9 * C) ** -0.5, 0.25)
    kernel_second = scatter_about(key_list[3], (3, 3, C, C), (9 * C) ** -0.5, 0.25)
    metric = jnp.clip(jnp.exp(jax.random.uniform(key_list[4], (LAT,), jnp.float32, math.log(0.5), math.log(3.0))), 0.5, 3.0)
    return {"fields": fields, "cotangent": cotangent, "kernel_first": kernel_first, "kernel_second": kernel_second, "metric": metric}


gelu_coef = 0.7978845608


def gelu_value(u):
    inner = jnp.tanh(gelu_coef * (u + 0.044715 * u * u * u))
    return 0.5 * u * (1.0 + inner)


def gelu_slope(u):
    inner = jnp.tanh(gelu_coef * (u + 0.044715 * u * u * u))
    return 0.5 * (1.0 + inner) + 0.5 * u * (1.0 - inner * inner) * gelu_coef * (1.0 + 3.0 * 0.044715 * u * u)


def pad_rows(value):
    return jnp.pad(value, ((0, 0), (0, 0), (1, 1)))


def stencil_apply(value, taps, metric):
    padded = pad_rows(value).astype(jnp.float32)
    total = jnp.zeros((taps.shape[2], value.shape[1], LAT), jnp.float32)
    for p in range(3):
        moved = jnp.roll(padded, -(p - 1), axis=1)
        summed = jnp.zeros_like(total)
        for q in range(3):
            summed = summed + jnp.einsum("oc,cij->oij", taps[p, q].astype(jnp.float32), moved[:, :, q:q + LAT])
        total = total + (summed if p == 1 else summed * metric[None, None, :])
    return total


def stencil_adjoint(plain, scaled, taps):
    total = jnp.zeros((taps.shape[3], plain.shape[1], LAT), jnp.float32)
    for p in range(3):
        source = pad_rows(plain if p == 1 else scaled).astype(jnp.float32)
        moved = jnp.roll(source, p - 1, axis=1)
        for q in range(3):
            total = total + jnp.einsum("oc,oij->cij", taps[p, q].astype(jnp.float32), moved[:, :, 2 - q:2 - q + LAT])
    return total


def kernel_term(plain, scaled, value):
    padded = pad_rows(value).astype(jnp.float32)
    terms = []
    for p in range(3):
        source = (plain if p == 1 else scaled).astype(jnp.float32)
        moved = jnp.roll(padded, -(p - 1), axis=1)
        row_terms = []
        for q in range(3):
            row_terms.append(jnp.einsum("oij,cij->oc", source, moved[:, :, q:q + LAT]))
        terms.append(jnp.stack(row_terms))
    return jnp.stack(terms)


def reference(fields, cotangent, kernel_first, kernel_second, metric):
    scale_row = metric[None, None, :]

    def one_sample(carry, pair):
        sample, upstream = pair
        before_gelu = stencil_apply(sample, kernel_first, metric)
        hidden = gelu_value(before_gelu).astype(jnp.bfloat16)
        upstream_scaled = (scale_row * upstream.astype(jnp.float32)).astype(jnp.bfloat16)
        second = kernel_term(upstream, upstream_scaled, hidden)
        hidden_grad = stencil_adjoint(upstream, upstream_scaled, kernel_second)
        delta = (hidden_grad * gelu_slope(before_gelu)).astype(jnp.bfloat16)
        delta_scaled = (scale_row * delta.astype(jnp.float32)).astype(jnp.bfloat16)
        first = kernel_term(delta, delta_scaled, sample)
        result = (upstream.astype(jnp.float32) + stencil_adjoint(delta, delta_scaled, kernel_first)).astype(jnp.bfloat16)
        return (carry[0] + first, carry[1] + second), result

    start = (jnp.zeros((3, 3, C, C), jnp.float32), jnp.zeros((3, 3, C, C), jnp.float32))
    sums, field_grad = lax.scan(one_sample, start, (fields, cotangent))
    factor = jnp.float32(1.0 / (float(SAMPLES) * float(LON) * float(LAT)) ** 0.5)
    return field_grad, (sums[0] * factor).astype(jnp.bfloat16), (sums[1] * factor).astype(jnp.bfloat16)
```

```python
import functools
import jax
import jax.numpy as jnp
from jax import lax
from jax.experimental import pallas as pl
from jax.experimental.pallas import tpu as pltpu
from jax.sharding import PartitionSpec as P

PLANE = 32
DEEP = 8
ROWS = 18
MESH = pl.DeviceIdType.MESH


def place():
    dp = lax.axis_index("dp")
    lon = lax.axis_index("lon")
    core = lon % 2
    z = (lon // 2) % DEEP
    high = lon // (2 * DEEP)
    return dp, lon, z, dp * 4 + high * 2 + core


def plane_device(member, z):
    return (member // 4, ((member // 2) % 2) * (2 * DEEP) + z * 2 + member % 2)


def greet():
    dp, lon, z, member = place()
    barrier = pltpu.get_barrier_semaphore()

    def to_plane(k, carry):
        peer = (member + k) % PLANE
        pl.semaphore_signal(barrier, inc=1, device_id=plane_device(peer, z), device_id_type=MESH)
        return carry

    def to_deep(k, carry):
        peer = (z + k) % DEEP
        pl.semaphore_signal(barrier, inc=1, device_id=plane_device(member, peer), device_id_type=MESH)
        return carry

    lax.fori_loop(1, PLANE, to_plane, 0)
    lax.fori_loop(1, DEEP, to_deep, 0)
    return barrier


def all_reduce(x_ref, factor, out, parts, zparts, whole, plane_send, plane_recv, deep_send, deep_recv, gather_send, gather_recv):
    dp, lon, z, member = place()
    for g in range(PLANE):
        out[g] = x_ref[g * ROWS:(g + 1) * ROWS, :].astype(out.dtype)

    def scatter(k):
        peer = (member + k) % PLANE
        back = (member + PLANE - k) % PLANE
        return pltpu.make_async_remote_copy(
            src_ref=out.at[peer], dst_ref=parts.at[member], send_sem=plane_send.at[peer], recv_sem=plane_recv.at[member],
            device_id=plane_device(peer, z), device_id_type=MESH)

    def arrive(k):
        peer = (member + k) % PLANE
        return pltpu.make_async_remote_copy(
            src_ref=out.at[peer], dst_ref=parts.at[peer], send_sem=plane_send.at[peer], recv_sem=plane_recv.at[peer],
            device_id=plane_device(peer, z), device_id_type=MESH)

    def run(start, stop, fn):
        def step(k, carry):
            fn(k)
            return carry
        lax.fori_loop(start, stop, step, 0)

    run(1, PLANE, lambda k: scatter(k).start())
    parts[member] = out[member]
    run(1, PLANE, lambda k: arrive(k).wait_recv())
    total = parts[0].astype(jnp.float32)
    for g in range(1, PLANE):
        total = total + parts[g].astype(jnp.float32)
    zparts[z] = total.astype(zparts.dtype)

    def deep(k):
        peer = (z + k) % DEEP
        return pltpu.make_async_remote_copy(
            src_ref=zparts.at[z], dst_ref=zparts.at[z], send_sem=deep_send.at[peer], recv_sem=deep_recv.at[z],
            device_id=plane_device(member, peer), device_id_type=MESH)

    def deep_in(k):
        peer = (z + k) % DEEP
        return pltpu.make_async_remote_copy(
            src_ref=zparts.at[z], dst_ref=zparts.at[peer], send_sem=deep_send.at[peer], recv_sem=deep_recv.at[peer],
            device_id=plane_device(member, peer), device_id_type=MESH)

    run(1, DEEP, lambda k: deep(k).start())
    run(1, DEEP, lambda k: deep_in(k).wait_recv())
    total = zparts[0].astype(jnp.float32)
    for g in range(1, DEEP):
        total = total + zparts[g].astype(jnp.float32)
    whole[member] = (total * factor).astype(whole.dtype)

    def gather(k):
        peer = (member + k) % PLANE
        return pltpu.make_async_remote_copy(
            src_ref=whole.at[member], dst_ref=whole.at[member], send_sem=gather_send.at[peer], recv_sem=gather_recv.at[member],
            device_id=plane_device(peer, z), device_id_type=MESH)

    def gathered(k):
        peer = (member + k) % PLANE
        return pltpu.make_async_remote_copy(
            src_ref=whole.at[member], dst_ref=whole.at[peer], send_sem=gather_send.at[peer], recv_sem=gather_recv.at[peer],
            device_id=plane_device(peer, z), device_id_type=MESH)

    run(1, PLANE, lambda k: gather(k).start())
    run(1, PLANE, lambda k: gathered(k).wait_recv())
    run(1, PLANE, lambda k: scatter(k).wait_send())
    run(1, DEEP, lambda k: deep(k).wait_send())
    run(1, PLANE, lambda k: gather(k).wait_send())


def reduce_kernel(factor, x_ref, y_ref, *scratch):
    barrier = greet()
    pl.semaphore_wait(barrier, PLANE + DEEP - 2)
    all_reduce(x_ref, factor, *scratch)
    whole = scratch[3]
    for g in range(PLANE):
        y_ref[g * ROWS:(g + 1) * ROWS, :] = whole[g].astype(jnp.float32)


def reduce_scratch():
    return [
        pltpu.VMEM((PLANE, ROWS, 128), jnp.bfloat16),
        pltpu.VMEM((PLANE, ROWS, 128), jnp.bfloat16),
        pltpu.VMEM((DEEP, ROWS, 128), jnp.float32),
        pltpu.VMEM((PLANE, ROWS, 128), jnp.bfloat16),
        pltpu.SemaphoreType.DMA((PLANE,)),
        pltpu.SemaphoreType.DMA((PLANE,)),
        pltpu.SemaphoreType.DMA((DEEP,)),
        pltpu.SemaphoreType.DMA((DEEP,)),
        pltpu.SemaphoreType.DMA((PLANE,)),
        pltpu.SemaphoreType.DMA((PLANE,)),
    ]


def reduced(grads, factor):
    return pl.pallas_call(
        functools.partial(reduce_kernel, factor),
        out_shape=jax.ShapeDtypeStruct((PLANE * ROWS, 128), jnp.float32),
        in_specs=[pl.BlockSpec(memory_space=pltpu.VMEM)],
        out_specs=pl.BlockSpec(memory_space=pltpu.VMEM),
        scratch_shapes=reduce_scratch(),
        compiler_params=pltpu.CompilerParams(collective_id=0, has_side_effects=True),
    )(grads)

gelu_coef = 0.7978845608


def extended(shard, sides, width):
    for axis, dim in sides:
        count, length = (lax.axis_size(axis), shard.shape[dim])
        up = [(i, (i + 1) % count) for i in range(count)]
        down = [(j, i) for i, j in up]
        last = lax.slice_in_dim(shard, length - width, length, axis=dim)
        first = lax.slice_in_dim(shard, 0, width, axis=dim)
        before = lax.ppermute(last, axis, up)
        after = lax.ppermute(first, axis, down)
        shard = jnp.concatenate([before, shard, after], axis=dim)
    return shard


def gelu_value(u):
    inner = jnp.tanh(gelu_coef * (u + 0.044715 * u * u * u))
    return 0.5 * u * (1.0 + inner)


def gelu_slope(u):
    inner = jnp.tanh(gelu_coef * (u + 0.044715 * u * u * u))
    return 0.5 * (1.0 + inner) + 0.5 * u * (1.0 - inner * inner) * gelu_coef * (
        1.0 + 3.0 * 0.044715 * u * u
    )


def pad_rows(value):
    return jnp.pad(value, ((0, 0), (0, 0), (0, 0), (1, 1)))


def stencil_apply(padded, taps, metric):
    columns = padded.shape[2] - 2
    lat_rows = padded.shape[3] - 2
    total = None
    for p in range(3):
        summed = None
        for q in range(3):
            term = jnp.einsum(
                "oc,bcij->boij",
                taps[p, q],
                padded[:, :, p : p + columns, q : q + lat_rows],
                preferred_element_type=jnp.float32,
            )
            summed = term if summed is None else summed + term
        summed = summed if p == 1 else summed * metric[None, None, None, :]
        total = summed if total is None else total + summed
    return total


def stencil_adjoint(plain_pad, scaled_pad, taps):
    columns = plain_pad.shape[2] - 2
    lat_rows = plain_pad.shape[3] - 2
    total = None
    for p in range(3):
        source = plain_pad if p == 1 else scaled_pad
        for q in range(3):
            term = jnp.einsum(
                "oc,boij->bcij",
                taps[p, q],
                source[:, :, 2 - p : 2 - p + columns, 2 - q : 2 - q + lat_rows],
                preferred_element_type=jnp.float32,
            )
            total = term if total is None else total + term
    return total


def kernel_term(plain, scaled, padded):
    columns = plain.shape[2]
    lat_rows = plain.shape[3]
    terms = []
    for p in range(3):
        source = plain if p == 1 else scaled
        row_terms = []
        for q in range(3):
            row_terms.append(
                jnp.einsum(
                    "boij,bcij->oc",
                    source,
                    padded[:, :, p : p + columns, q : q + lat_rows],
                    preferred_element_type=jnp.float32,
                )
            )
        terms.append(jnp.stack(row_terms))
    return jnp.stack(terms)


def per_device(fields, cotangent, kernel_first, kernel_second, metric):
    metric_padded = jnp.pad(metric, (1, 1))[None, None, None, :]
    samples_here = fields.shape[0]
    stacked = jnp.concatenate((fields, cotangent), axis=0)
    both_pad = extended(stacked, (("lon", 2),), 1)
    input_pad = pad_rows(both_pad[:samples_here])
    upstream_pad = pad_rows(both_pad[samples_here:])
    before_gelu = stencil_apply(input_pad, kernel_first, metric)
    hidden = gelu_value(before_gelu).astype(jnp.bfloat16)
    hidden_pad = pad_rows(extended(hidden, (("lon", 2),), 1))
    scaled_pad = (metric_padded * upstream_pad.astype(jnp.float32)).astype(jnp.bfloat16)
    second = kernel_term(cotangent, scaled_pad[:, :, 1:-1, 1:-1], hidden_pad)
    hidden_grad = stencil_adjoint(upstream_pad, scaled_pad, kernel_second)
    delta = (hidden_grad * gelu_slope(before_gelu)).astype(jnp.bfloat16)
    delta_pad = pad_rows(extended(delta, (("lon", 2),), 1))
    delta_scaled = (metric_padded * delta_pad.astype(jnp.float32)).astype(jnp.bfloat16)
    field_grad = (
        cotangent.astype(jnp.float32) + stencil_adjoint(delta_pad, delta_scaled, kernel_first)
    ).astype(jnp.bfloat16)
    first = kernel_term(delta, delta_scaled[:, :, 1:-1, 1:-1], input_pad)
    counted = (
        float(fields.shape[0] * lax.axis_size("dp"))
        * float(fields.shape[2] * lax.axis_size("lon"))
        * float(fields.shape[3])
    )
    both = jnp.stack((first, second))
    done = reduced(both.reshape(PLANE * ROWS, 128), 1.0 / counted**0.5)
    done = done.reshape(both.shape).astype(jnp.bfloat16)
    return field_grad, done[0], done[1]


def solution(mesh):
    placed = (P("dp", None, "lon", None), P("dp", None, "lon", None), P(), P(), P())
    return jax.shard_map(
        per_device,
        mesh=mesh,
        in_specs=placed,
        out_specs=(P("dp", None, "lon", None), P(), P()),
        check_vma=False,
    )
```

```python
import functools
import jax
import jax.numpy as jnp
from jax import lax
from jax.experimental import pallas as pl
from jax.experimental.pallas import tpu as pltpu
from jax.sharding import PartitionSpec as P

MESH = pl.DeviceIdType.MESH
TOTAL_ROWS = 576


class Grid:
    def __init__(self, dp_size, lon_size):
        self.high = 2 if lon_size == 32 else 1
        self.deep = lon_size // (2 * self.high)
        self.plane = dp_size * self.high * 2
        self.rows = TOTAL_ROWS // self.plane

    def place(self):
        dp = lax.axis_index("dp")
        lon = lax.axis_index("lon")
        core = lon % 2
        z = (lon // 2) % self.deep
        high = lon // (2 * self.deep)
        return dp, lon, z, (dp * self.high + high) * 2 + core

    def device(self, member, z):
        high = (member // 2) % self.high
        return (member // (2 * self.high), (high * self.deep + z) * 2 + member % 2)

    def greeted(self):
        return self.plane + self.deep - 2

    def greet(self):
        dp, lon, z, member = self.place()
        barrier = pltpu.get_barrier_semaphore()

        def signal(device):
            pl.semaphore_signal(barrier, inc=1, device_id=device, device_id_type=MESH)

        loop(1, self.plane, lambda k: signal(self.device((member + k) % self.plane, z)))
        loop(1, self.deep, lambda k: signal(self.device(member, (z + k) % self.deep)))
        return barrier


class Reduction:
    def __init__(self, grid, flat, factor, out, parts, zparts, whole, plane_send, plane_recv, deep_send, deep_recv, gather_send, gather_recv):
        self.grid, self.flat, self.factor = grid, flat, factor
        self.out, self.parts, self.zparts, self.whole = out, parts, zparts, whole
        self.plane_send, self.plane_recv = plane_send, plane_recv
        self.deep_send, self.deep_recv = deep_send, deep_recv
        self.gather_send, self.gather_recv = gather_send, gather_recv
        self.dp, self.lon, self.z, self.member = grid.place()

    def scatter(self, k, slot):
        peer = (self.member + k) % self.grid.plane
        slot = self.member if slot is None else peer
        return pltpu.make_async_remote_copy(
            src_ref=self.out.at[peer], dst_ref=self.parts.at[slot], send_sem=self.plane_send.at[peer],
            recv_sem=self.plane_recv.at[slot], device_id=self.grid.device(peer, self.z), device_id_type=MESH)

    def across(self, k, slot):
        peer = (self.z + k) % self.grid.deep
        slot = self.z if slot is None else peer
        return pltpu.make_async_remote_copy(
            src_ref=self.zparts.at[self.z], dst_ref=self.zparts.at[slot], send_sem=self.deep_send.at[peer],
            recv_sem=self.deep_recv.at[slot], device_id=self.grid.device(self.member, peer), device_id_type=MESH)

    def gather(self, k, slot):
        peer = (self.member + k) % self.grid.plane
        slot = self.member if slot is None else peer
        return pltpu.make_async_remote_copy(
            src_ref=self.whole.at[self.member], dst_ref=self.whole.at[slot], send_sem=self.gather_send.at[peer],
            recv_sem=self.gather_recv.at[slot], device_id=self.grid.device(peer, self.z), device_id_type=MESH)

    def scatter_start(self):
        rows = self.grid.rows
        for g in range(self.grid.plane):
            self.out[g] = self.flat[g * rows:(g + 1) * rows, :].astype(self.out.dtype)
        self.parts[self.member] = self.out[self.member]
        loop(1, self.grid.plane, lambda k: self.scatter(k, None).start())

    def finish(self):
        plane, deep, rows = self.grid.plane, self.grid.deep, self.grid.rows
        loop(1, plane, lambda k: self.scatter(k, 0).wait_recv())
        total = self.parts[0].astype(F32)
        for g in range(1, plane):
            total = total + self.parts[g].astype(F32)
        self.zparts[self.z] = total.astype(self.zparts.dtype)
        loop(1, deep, lambda k: self.across(k, None).start())
        loop(1, deep, lambda k: self.across(k, 0).wait_recv())
        total = self.zparts[0].astype(F32)
        for g in range(1, deep):
            total = total + self.zparts[g].astype(F32)
        self.whole[self.member] = (total * self.factor).astype(self.whole.dtype)
        loop(1, plane, lambda k: self.gather(k, None).start())
        loop(1, plane, lambda k: self.gather(k, 0).wait_recv())
        for g in range(plane):
            self.flat[g * rows:(g + 1) * rows, :] = self.whole[g].astype(F32)
        loop(1, plane, lambda k: self.scatter(k, None).wait_send())
        loop(1, deep, lambda k: self.across(k, None).wait_send())
        loop(1, plane, lambda k: self.gather(k, None).wait_send())


def net_scratch(grid):
    return [
        pltpu.VMEM((grid.plane, grid.rows, 128), BF16),
        pltpu.VMEM((grid.plane, grid.rows, 128), BF16),
        pltpu.VMEM((grid.deep, grid.rows, 128), F32),
        pltpu.VMEM((grid.plane, grid.rows, 128), BF16),
        pltpu.SemaphoreType.DMA((grid.plane,)),
        pltpu.SemaphoreType.DMA((grid.plane,)),
        pltpu.SemaphoreType.DMA((grid.deep,)),
        pltpu.SemaphoreType.DMA((grid.deep,)),
        pltpu.SemaphoreType.DMA((grid.plane,)),
        pltpu.SemaphoreType.DMA((grid.plane,)),
    ]


C = 64
COLS = 16
LAT = 384
SLOTS = COLS + 4
gelu_coef = 0.7978845608
F32 = jnp.float32
BF16 = jnp.bfloat16
NT = (((1,), (1,)), ((), ()))


def loop(start, stop, fn):
    def step(k, carry):
        fn(k)
        return carry

    lax.fori_loop(start, stop, step, 0)


def moved_rows(x):
    lane = lax.broadcasted_iota(jnp.int32, x.shape, 1)
    zero = jnp.zeros_like(x)
    right = jnp.where(lane == 0, zero, pltpu.roll(x, 1, 1))
    left = jnp.where(lane == LAT - 1, zero, pltpu.roll(x, LAT - 1, 1))
    return jnp.concatenate([right, x, left], axis=0)


def dot(a, b):
    return jnp.dot(a, b, preferred_element_type=F32)


def adjoint_taps(k_ref, p):
    row = lax.broadcasted_iota(jnp.int32, (C, C), 0)
    col = lax.broadcasted_iota(jnp.int32, (C, C), 1)
    one = jnp.where(row == col, 1.0, 0.0).astype(BF16)
    stacked = jnp.concatenate([k_ref[p, 2], k_ref[p, 1], k_ref[p, 0]], axis=0)
    return lax.dot_general(one, stacked, NT, preferred_element_type=F32).astype(BF16)


def step_kernel(grid, factor, f_ref, t_ref, k1_ref, k2_ref, m_ref, out_ref, g1_ref, g2_ref,
                ft, tt, ts, f3, y, z, hid, d, ds, taps, near, far, acc, flat,
                halo_send, halo_recv, *net):
    dp, lon, deep, member = grid.place()
    lon_size = lax.axis_size("lon")
    right = (dp, (lon + 1) % lon_size)
    left = (dp, (lon + lon_size - 1) % lon_size)
    barrier = grid.greet()
    for neighbour in (left, right):
        pl.semaphore_signal(barrier, inc=1, device_id=neighbour, device_id_type=MESH)

    def turn(k):
        rows = pl.ds(pl.multiple_of(k * 16, 16), 16)
        ft[2:2 + COLS, rows, :] = jnp.swapaxes(f_ref[rows], 0, 1)
        tt[2:2 + COLS, rows, :] = jnp.swapaxes(t_ref[rows], 0, 1)

    loop(0, C // 16, turn)
    pl.semaphore_wait(barrier, grid.greeted() + 2)
    copies = []
    for index, ref in enumerate((ft, tt)):
        copies.append(pltpu.make_async_remote_copy(
            src_ref=ref.at[pl.ds(COLS, 2)], dst_ref=ref.at[pl.ds(0, 2)], send_sem=halo_send.at[2 * index],
            recv_sem=halo_recv.at[2 * index], device_id=right, device_id_type=MESH))
        copies.append(pltpu.make_async_remote_copy(
            src_ref=ref.at[pl.ds(2, 2)], dst_ref=ref.at[pl.ds(COLS + 2, 2)], send_sem=halo_send.at[2 * index + 1],
            recv_sem=halo_recv.at[2 * index + 1], device_id=left, device_id_type=MESH))
    for copy in copies:
        copy.start()

    for p in range(3):
        taps[p * C:(p + 1) * C, :] = jnp.concatenate([k1_ref[p, 0], k1_ref[p, 1], k1_ref[p, 2]], axis=1)
    for index, k_ref in enumerate((k1_ref, k2_ref)):
        far[index] = jnp.concatenate([adjoint_taps(k_ref, 0), adjoint_taps(k_ref, 2)], axis=0)
        near[index] = adjoint_taps(k_ref, 1)
    metric = m_ref[...]

    def adjoint_block(index, slot, count, plain, scaled):
        p3 = jnp.concatenate([moved_rows(v) for v in plain], axis=1)
        s3 = jnp.concatenate([moved_rows(v) for v in scaled], axis=1)
        zn = dot(near[index], p3)
        zf = dot(far[index], s3)
        for n in range(count):
            z[slot + n, :2 * C] = zf[:, n * LAT:(n + 1) * LAT]
            z[slot + n, 2 * C:] = zn[:, n * LAT:(n + 1) * LAT]

    def first_block(slot, count):
        rows = []
        plain = []
        scaled = []
        for n in range(count):
            rows.append(moved_rows(ft[slot + n]))
            f3[slot + n] = rows[n]
            plain.append(tt[slot + n])
            scaled.append((plain[n].astype(F32) * metric).astype(BF16))
            ts[slot + n] = scaled[n]
        yb = dot(taps[...], jnp.concatenate(rows, axis=1))
        for n in range(count):
            y[slot + n] = yb[:, n * LAT:(n + 1) * LAT]
        adjoint_block(1, slot, count, plain, scaled)

    loop(0, 4, lambda b: first_block(2 + 4 * b, 4))
    for copy in copies:
        copy.wait_recv()
    loop(0, 2, lambda b: first_block((COLS + 2) * b, 2))

    def adjoint_sum(s):
        return z[s, 2 * C:] + z[s - 1, C:2 * C] + z[s + 1, :C]

    def middle(s):
        u = y[s, C:2 * C] + metric * (y[s - 1, :C] + y[s + 1, 2 * C:])
        square = u * u
        inner = jnp.tanh(gelu_coef * (u + 0.044715 * square * u))
        half = 0.5 * (1.0 + inner)
        slope = half + (0.5 * gelu_coef) * u * (1.0 - inner * inner) * (1.0 + 3.0 * 0.044715 * square)
        hid[s] = (u * half).astype(BF16)
        delta = (adjoint_sum(s) * slope).astype(BF16)
        d[s] = delta
        ds[s] = (delta.astype(F32) * metric).astype(BF16)

    def middle_two(b):
        middle(1 + 2 * b)
        middle(2 + 2 * b)

    loop(0, (COLS + 2) // 2, middle_two)

    acc[...] = jnp.zeros_like(acc)

    def gradient(b):
        s = 2 + 4 * b
        h3 = jnp.concatenate([moved_rows(hid[s + n]) for n in range(4)], axis=1)
        e3 = jnp.concatenate([
            jnp.concatenate([ts[s + n + 1], tt[s + n], ts[s + n - 1]], axis=0) for n in range(4)], axis=1)
        acc[1] += lax.dot_general(e3, h3, NT, preferred_element_type=F32)
        v3 = jnp.concatenate([f3[s + n] for n in range(4)], axis=1)
        d3 = jnp.concatenate([
            jnp.concatenate([ds[s + n + 1], d[s + n], ds[s + n - 1]], axis=0) for n in range(4)], axis=1)
        acc[0] += lax.dot_general(d3, v3, NT, preferred_element_type=F32)

    loop(0, 4, gradient)
    for index in range(2):
        flat[index * 192:(index + 1) * 192, :] = acc[index, :, :128]
        flat[384 + index * 96:384 + (index + 1) * 96, :] = jnp.concatenate(
            [acc[index, :96, 128:], acc[index, 96:, 128:]], axis=1)
    reduction = Reduction(grid, flat, factor, *net)
    reduction.scatter_start()

    def last_block(slot, count):
        adjoint_block(0, slot, count, [d[slot + n] for n in range(count)], [ds[slot + n] for n in range(count)])

    loop(0, 6, lambda b: last_block(1 + 3 * b, 3))

    def finish(s):
        tt[s] = (tt[s].astype(F32) + adjoint_sum(s)).astype(BF16)

    def finish_two(b):
        finish(2 + 2 * b)
        finish(3 + 2 * b)

    for copy in copies:
        copy.wait_send()
    loop(0, COLS // 2, finish_two)

    def turn_back(k):
        rows = pl.ds(pl.multiple_of(k * 16, 16), 16)
        out_ref[rows] = jnp.swapaxes(tt[2:2 + COLS, rows, :], 0, 1)

    loop(0, C // 16, turn_back)
    reduction.finish()
    for index, g_ref in enumerate((g1_ref, g2_ref)):
        for p in range(3):
            base = index * 192 + p * C
            pair = flat[base:base + C, :]
            g_ref[p, 0] = pair[:, :C].astype(BF16)
            g_ref[p, 1] = pair[:, C:].astype(BF16)
        side = flat[384 + index * 96:384 + (index + 1) * 96, :]
        rest = jnp.concatenate([side[:, :C], side[:, C:]], axis=0)
        for p in range(3):
            g_ref[p, 2] = rest[p * C:(p + 1) * C].astype(BF16)


def per_device(fields, cotangent, kernel_first, kernel_second, metric):
    dp_size, lon_size = lax.axis_size("dp"), lax.axis_size("lon")
    grid = Grid(dp_size, lon_size)
    factor = 1.0 / (float(dp_size) * float(COLS * lon_size) * float(LAT)) ** 0.5
    vmem = pl.BlockSpec(memory_space=pltpu.VMEM)
    field_grad, first, second = pl.pallas_call(
        functools.partial(step_kernel, grid, factor),
        out_shape=(
            jax.ShapeDtypeStruct((C, COLS, LAT), BF16),
            jax.ShapeDtypeStruct((3, 3, C, C), BF16),
            jax.ShapeDtypeStruct((3, 3, C, C), BF16),
        ),
        in_specs=[vmem] * 5,
        out_specs=(vmem, vmem, vmem),
        scratch_shapes=[
            pltpu.VMEM((SLOTS, C, LAT), BF16),
            pltpu.VMEM((SLOTS, C, LAT), BF16),
            pltpu.VMEM((SLOTS, C, LAT), BF16),
            pltpu.VMEM((SLOTS, 3 * C, LAT), BF16),
            pltpu.VMEM((SLOTS, 3 * C, LAT), F32),
            pltpu.VMEM((SLOTS, 3 * C, LAT), F32),
            pltpu.VMEM((SLOTS, C, LAT), BF16),
            pltpu.VMEM((SLOTS, C, LAT), BF16),
            pltpu.VMEM((SLOTS, C, LAT), BF16),
            pltpu.VMEM((3 * C, 3 * C), BF16),
            pltpu.VMEM((2, C, 3 * C), BF16),
            pltpu.VMEM((2, 2 * C, 3 * C), BF16),
            pltpu.VMEM((2, 3 * C, 3 * C), F32),
            pltpu.VMEM((TOTAL_ROWS, 128), F32),
            pltpu.SemaphoreType.DMA((4,)),
            pltpu.SemaphoreType.DMA((4,)),
        ] + net_scratch(grid),
        compiler_params=pltpu.CompilerParams(
            collective_id=0, has_side_effects=True, vmem_limit_bytes=56 * 2**20),
    )(fields[0], cotangent[0], kernel_first, kernel_second, metric[None, :])
    return field_grad[None], first, second


def solution(mesh):
    placed = (P("dp", None, "lon", None), P("dp", None, "lon", None), P(), P(), P())
    return jax.shard_map(
        per_device,
        mesh=mesh,
        in_specs=placed,
        out_specs=(P("dp", None, "lon", None), P(), P()),
        check_vma=False,
    )
```

```python
import functools
import jax
import jax.numpy as jnp
from jax import lax
from jax.experimental import pallas as pl
from jax.experimental.pallas import tpu as pltpu
from jax.sharding import PartitionSpec as P

MESH = pl.DeviceIdType.MESH
TOTAL_ROWS = 576
GRAD_ROWS = 288
C = 64
COLS = 16
LAT = 384
SLOTS = COLS + 4
gelu_coef = 0.7978845608
F32 = jnp.float32
BF16 = jnp.bfloat16
NT = (((1,), (1,)), ((), ()))


def loop(start, stop, fn):
    def step(k, carry):
        fn(k)
        return carry

    lax.fori_loop(start, stop, step, 0)


class Grid:
    def __init__(self, dp_size, lon_size):
        self.high = 2 if lon_size == 32 else 1
        self.deep = lon_size // (2 * self.high)
        self.wide = dp_size // 2
        self.tall = 2 * self.high
        self.plane = 2 * self.wide * self.tall
        self.rows = TOTAL_ROWS // self.plane

    def place(self):
        dp = lax.axis_index("dp")
        lon = lax.axis_index("lon")
        x = lax.rem(dp, self.wide)
        y = lax.div(lon, 2 * self.deep) * 2 + lax.div(dp, self.wide)
        z = lax.rem(lax.div(lon, 2), self.deep)
        return x, y, z, lax.rem(lon, 2)

    def device(self, x, y, z, core):
        return (lax.rem(y, 2) * self.wide + x, (lax.div(y, 2) * self.deep + z) * 2 + core)

    def member(self, m, z):
        x = lax.rem(lax.div(m, self.tall), self.wide)
        return self.device(x, lax.rem(m, self.tall), z, lax.div(m, self.wide * self.tall))

    def own(self):
        x, y, z, core = self.place()
        return (core * self.wide + x) * self.tall + y, z

    def greet(self, barrier):
        m, z = self.own()

        def signal(device):
            pl.semaphore_signal(barrier, inc=1, device_id=device, device_id_type=MESH)

        loop(1, self.plane, lambda k: signal(self.member(lax.rem(m + k, self.plane), z)))
        loop(1, self.deep, lambda k: signal(self.member(m, lax.rem(z + k, self.deep))))
        return self.plane + self.deep - 2


def send(src, dst, send_sem, recv_sem, device):
    return pltpu.make_async_remote_copy(
        src_ref=src, dst_ref=dst, send_sem=send_sem, recv_sem=recv_sem, device_id=device, device_id_type=MESH)


class Reduction:
    def __init__(self, grid, factor, out, parts, zparts, whole, plane_sem, deep_sem, gather_sem):
        self.grid, self.factor = grid, factor
        self.out, self.parts, self.zparts, self.whole = out, parts, zparts, whole
        self.plane_sem, self.deep_sem, self.gather_sem = plane_sem, deep_sem, gather_sem
        self.m, self.z = grid.own()

    def scatter(self, k, arrival=False):
        peer = lax.rem(self.m + k, self.grid.plane)
        slot = peer if arrival else self.m
        return send(self.out.at[peer], self.parts.at[slot], self.plane_sem.at[0, peer], self.plane_sem.at[1, slot],
                    self.grid.member(peer, self.z))

    def across(self, k, arrival=False):
        peer = lax.rem(self.z + k, self.grid.deep)
        slot = peer if arrival else self.z
        return send(self.zparts.at[self.z], self.zparts.at[slot], self.deep_sem.at[0, peer], self.deep_sem.at[1, slot],
                    self.grid.member(self.m, peer))

    def gather(self, k, arrival=False):
        peer = lax.rem(self.m + k, self.grid.plane)
        slot = peer if arrival else self.m
        return send(self.whole.at[self.m], self.whole.at[slot], self.gather_sem.at[0, peer], self.gather_sem.at[1, slot],
                    self.grid.member(peer, self.z))

    def start(self, flat):
        rows = self.grid.rows
        for g in range(self.grid.plane):
            self.out[g] = flat[g * rows:(g + 1) * rows, :].astype(BF16)
        loop(1, self.grid.plane, lambda k: self.scatter(k).start())
        self.parts[self.m] = self.out[self.m]

    def finish(self):
        plane, deep = self.grid.plane, self.grid.deep
        loop(1, plane, lambda k: self.scatter(k, True).wait_recv())
        total = self.parts[0].astype(F32)
        for g in range(1, plane):
            total = total + self.parts[g].astype(F32)
        self.zparts[self.z] = total
        loop(1, deep, lambda k: self.across(k).start())
        loop(1, deep, lambda k: self.across(k, True).wait_recv())
        total = self.zparts[0]
        for g in range(1, deep):
            total = total + self.zparts[g]
        self.whole[self.m] = (total * self.factor).astype(BF16)
        loop(1, plane, lambda k: self.gather(k).start())
        loop(1, plane, lambda k: self.scatter(k).wait_send())
        loop(1, deep, lambda k: self.across(k).wait_send())
        loop(1, plane, lambda k: self.gather(k, True).wait_recv())
        loop(1, plane, lambda k: self.gather(k).wait_send())


def net_scratch(grid):
    block = (grid.rows, 128)
    return [
        pltpu.VMEM((grid.plane,) + block, BF16),
        pltpu.VMEM((grid.plane,) + block, BF16),
        pltpu.VMEM((grid.deep,) + block, F32),
        pltpu.VMEM((grid.plane,) + block, BF16),
        pltpu.SemaphoreType.DMA((2, grid.plane)),
        pltpu.SemaphoreType.DMA((2, grid.deep)),
        pltpu.SemaphoreType.DMA((2, grid.plane)),
    ]


def moved_rows(x):
    lane = lax.broadcasted_iota(jnp.int32, x.shape, 1)
    zero = jnp.zeros_like(x)
    right = jnp.where(lane == 0, zero, pltpu.roll(x, 1, 1))
    left = jnp.where(lane == LAT - 1, zero, pltpu.roll(x, LAT - 1, 1))
    return jnp.concatenate([right, x, left], axis=0)


def dot(a, b):
    return jnp.dot(a, b, preferred_element_type=F32)


def adjoint_taps(k_ref, p):
    row = lax.broadcasted_iota(jnp.int32, (C, C), 0)
    col = lax.broadcasted_iota(jnp.int32, (C, C), 1)
    one = jnp.where(row == col, 1.0, 0.0).astype(BF16)
    stacked = jnp.concatenate([k_ref[p, 2], k_ref[p, 1], k_ref[p, 0]], axis=0)
    return lax.dot_general(one, stacked, NT, preferred_element_type=F32).astype(BF16)


def step_kernel(grid, factor, f_any, t_any, k1_any, k2_any, m_any, out_ref, g_ref,
                f_ref, t_ref, k1_ref, k2_ref, m_ref,
                ft, tt, ts, f3, y, z, hid, d, ds, fg, taps, near, far, acc, flat,
                load_sem, halo_send, halo_recv, *net):
    loads = [pltpu.make_async_copy(source, target, load_sem.at[n]) for n, (source, target) in enumerate(
        ((f_any, f_ref), (t_any, t_ref), (k1_any, k1_ref), (k2_any, k2_ref), (m_any, m_ref)))]
    for load in loads:
        load.start()
    dp, lon = lax.axis_index("dp"), lax.axis_index("lon")
    lon_size = lax.axis_size("lon")
    right = (dp, lax.rem(lon + 1, lon_size))
    left = (dp, lax.rem(lon + lon_size - 1, lon_size))
    barrier = pltpu.get_barrier_semaphore()
    for peer in (left, right):
        pl.semaphore_signal(barrier, inc=1, device_id=peer, device_id_type=MESH)
    greeted = 2 + grid.greet(barrier)

    def turner(source, target):
        def turn(k):
            rows = pl.ds(pl.multiple_of(k * 16, 16), 16)
            target[2:2 + COLS, rows, :] = jnp.swapaxes(source[rows], 0, 1)
        return turn

    loads[0].wait()
    loop(0, C // 16, turner(f_ref, ft))
    loads[1].wait()
    loop(0, C // 16, turner(t_ref, tt))
    pl.semaphore_wait(barrier, greeted)
    copies = []
    for index, ref in enumerate((ft, tt)):
        copies.append(send(ref.at[pl.ds(COLS, 2)], ref.at[pl.ds(0, 2)],
                           halo_send.at[2 * index], halo_recv.at[2 * index], right))
        copies.append(send(ref.at[pl.ds(2, 2)], ref.at[pl.ds(COLS + 2, 2)],
                           halo_send.at[2 * index + 1], halo_recv.at[2 * index + 1], left))
    for copy in copies:
        copy.start()

    for load in loads[2:]:
        load.wait()
    for p in range(3):
        taps[p * C:(p + 1) * C, :] = jnp.concatenate([k1_ref[p, 0], k1_ref[p, 1], k1_ref[p, 2]], axis=1)
    for index, k_ref in enumerate((k1_ref, k2_ref)):
        far[index] = jnp.concatenate([adjoint_taps(k_ref, 0), adjoint_taps(k_ref, 2)], axis=0)
        near[index] = adjoint_taps(k_ref, 1)
    metric = m_ref[...].reshape(1, LAT)

    def adjoint_block(index, slots, plain, scaled):
        p3 = jnp.concatenate([moved_rows(v) for v in plain], axis=1)
        s3 = jnp.concatenate([moved_rows(v) for v in scaled], axis=1)
        zn = dot(near[index], p3)
        zf = dot(far[index], s3)
        for n, s in enumerate(slots):
            z[s, :2 * C] = zf[:, n * LAT:(n + 1) * LAT]
            z[s, 2 * C:] = zn[:, n * LAT:(n + 1) * LAT]

    def first_block(slots):
        rows = [moved_rows(ft[s]) for s in slots]
        plain = [tt[s] for s in slots]
        scaled = [(v.astype(F32) * metric).astype(BF16) for v in plain]
        for n, s in enumerate(slots):
            f3[s] = rows[n]
            ts[s] = scaled[n]
        yb = dot(taps[...], jnp.concatenate(rows, axis=1))
        for n, s in enumerate(slots):
            y[s] = yb[:, n * LAT:(n + 1) * LAT]
        adjoint_block(1, slots, plain, scaled)

    def adjoint_sum(s):
        return z[s, 2 * C:] + z[s - 1, C:2 * C] + z[s + 1, :C]

    def middle(s):
        u = y[s, C:2 * C] + metric * (y[s - 1, :C] + y[s + 1, 2 * C:])
        square = u * u
        inner = jnp.tanh(gelu_coef * (u + 0.044715 * square * u))
        half = 0.5 * (1.0 + inner)
        slope = half + (0.5 * gelu_coef) * u * (1.0 - inner * inner) * (1.0 + 3.0 * 0.044715 * square)
        hid[s] = (u * half).astype(BF16)
        delta = (adjoint_sum(s) * slope).astype(BF16)
        d[s] = delta
        ds[s] = (delta.astype(F32) * metric).astype(BF16)

    def middle_two(s):
        middle(s)
        middle(s + 1)

    def trio(plain, scaled, s):
        return jnp.concatenate([scaled[s + 1], plain[s], scaled[s - 1]], axis=0)

    def second_term(slots):
        h3 = jnp.concatenate([moved_rows(hid[s]) for s in slots], axis=1)
        e3 = jnp.concatenate([trio(tt, ts, s) for s in slots], axis=1)
        acc[1] += lax.dot_general(e3, h3, NT, preferred_element_type=F32)

    def first_term(slots):
        v3 = jnp.concatenate([f3[s] for s in slots], axis=1)
        d3 = jnp.concatenate([trio(d, ds, s) for s in slots], axis=1)
        acc[0] += lax.dot_general(d3, v3, NT, preferred_element_type=F32)

    def terms(b):
        second_term([3 + 7 * b + n for n in range(7)])
        first_term([4 + 6 * b + n for n in range(6)])

    acc[...] = jnp.zeros_like(acc)
    loop(0, 4, lambda b: first_block([2 + 4 * b + n for n in range(4)]))
    loop(0, 7, lambda b: middle_two(3 + 2 * b))
    loop(0, 2, terms)
    for copy in copies:
        copy.wait_recv()
    first_block([0, 1, COLS + 2, COLS + 3])
    middle_two(1)
    middle_two(COLS + 1)
    second_term([2, COLS + 1])
    first_term([2, 3, COLS, COLS + 1])

    reduction = Reduction(grid, factor, *net)
    for index in range(2):
        flat[index * GRAD_ROWS:index * GRAD_ROWS + 192, :] = acc[index, :, :128]
        flat[index * GRAD_ROWS + 192:(index + 1) * GRAD_ROWS, :] = jnp.concatenate(
            [acc[index, :96, 128:], acc[index, 96:, 128:]], axis=1)
    reduction.start(flat)

    def last_block(b):
        slots = [1 + 3 * b + n for n in range(3)]
        adjoint_block(0, slots, [d[s] for s in slots], [ds[s] for s in slots])

    def finish(s):
        fg[s - 2] = (tt[s].astype(F32) + adjoint_sum(s)).astype(BF16)

    def finish_two(b):
        finish(2 + 2 * b)
        finish(3 + 2 * b)

    def turn_back(k):
        part = pl.ds(pl.multiple_of(k * 16, 16), 16)
        out_ref[part] = jnp.swapaxes(fg[:, part, :], 0, 1)

    loop(0, 6, last_block)
    loop(0, COLS // 2, finish_two)
    loop(0, C // 16, turn_back)
    for copy in copies:
        copy.wait_send()
    reduction.finish()
    g_ref[...] = reduction.whole[...]


def format_kernel(grid, x_ref, g_ref, out_ref, g1_ref, g2_ref, flat, sem):
    copy = pltpu.make_async_copy(x_ref, out_ref, sem)
    copy.start()
    rows = grid.rows
    for g in range(TOTAL_ROWS // rows):
        flat[g * rows:(g + 1) * rows, :] = g_ref[g].astype(F32)
    for index, ref in enumerate((g1_ref, g2_ref)):
        for p in range(3):
            base = index * GRAD_ROWS + p * C
            pair = flat[base:base + C, :]
            ref[p, 0] = pair[:, :C].astype(BF16)
            ref[p, 1] = pair[:, C:].astype(BF16)
        side = flat[index * GRAD_ROWS + 192:(index + 1) * GRAD_ROWS, :]
        rest = jnp.concatenate([side[:, :C], side[:, C:]], axis=0)
        for p in range(3):
            ref[p, 2] = rest[p * C:(p + 1) * C].astype(BF16)
    copy.wait()


def per_device(fields, cotangent, kernel_first, kernel_second, metric):
    dp_size, lon_size = lax.axis_size("dp"), lax.axis_size("lon")
    grid = Grid(dp_size, lon_size)
    factor = 1.0 / (float(dp_size) * float(COLS * lon_size) * float(LAT)) ** 0.5
    vmem = pl.BlockSpec(memory_space=pltpu.VMEM)
    anywhere = pl.BlockSpec(memory_space=pl.ANY)
    taps = (3, 3, C, C)
    column = pltpu.VMEM((SLOTS, C, LAT), BF16)
    turned, packed = pl.pallas_call(
        functools.partial(step_kernel, grid, factor),
        out_shape=(
            pltpu.VMEM((C, COLS, LAT), BF16),
            pltpu.VMEM((grid.plane, grid.rows, 128), BF16),
        ),
        in_specs=[anywhere] * 5,
        out_specs=(vmem, vmem),
        scratch_shapes=[
            pltpu.VMEM((C, COLS, LAT), BF16),
            pltpu.VMEM((C, COLS, LAT), BF16),
            pltpu.VMEM(taps, BF16),
            pltpu.VMEM(taps, BF16),
            pltpu.VMEM((LAT,), F32),
            column,
            column,
            column,
            pltpu.VMEM((SLOTS, 3 * C, LAT), BF16),
            pltpu.VMEM((SLOTS, 3 * C, LAT), F32),
            pltpu.VMEM((SLOTS, 3 * C, LAT), F32),
            column,
            column,
            column,
            pltpu.VMEM((COLS, C, LAT), BF16),
            pltpu.VMEM((3 * C, 3 * C), BF16),
            pltpu.VMEM((2, C, 3 * C), BF16),
            pltpu.VMEM((2, 2 * C, 3 * C), BF16),
            pltpu.VMEM((2, 3 * C, 3 * C), F32),
            pltpu.VMEM((TOTAL_ROWS, 128), F32),
            pltpu.SemaphoreType.DMA((5,)),
            pltpu.SemaphoreType.DMA((4,)),
            pltpu.SemaphoreType.DMA((4,)),
        ] + net_scratch(grid),
        compiler_params=pltpu.CompilerParams(
            collective_id=0, has_side_effects=True, vmem_limit_bytes=60 * 2**20),
    )(fields[0], cotangent[0], kernel_first, kernel_second, metric)
    field_grad, first, second = pl.pallas_call(
        functools.partial(format_kernel, grid),
        out_shape=(
            jax.ShapeDtypeStruct((C, COLS, LAT), BF16),
            jax.ShapeDtypeStruct(taps, BF16),
            jax.ShapeDtypeStruct(taps, BF16),
        ),
        in_specs=[vmem, vmem],
        out_specs=(anywhere, vmem, vmem),
        scratch_shapes=[pltpu.VMEM((TOTAL_ROWS, 128), F32), pltpu.SemaphoreType.DMA(())],
        compiler_params=pltpu.CompilerParams(vmem_limit_bytes=16 * 2**20),
    )(turned, packed)
    return field_grad[None], first, second


def solution(mesh):
    placed = (P("dp", None, "lon", None), P("dp", None, "lon", None), P(), P(), P())
    return jax.shard_map(
        per_device,
        mesh=mesh,
        in_specs=placed,
        out_specs=(P("dp", None, "lon", None), P(), P()),
        check_vma=False,
    )
```

```python
import functools
import jax
import jax.numpy as jnp
from jax import lax
from jax.experimental import pallas as pl
from jax.experimental.pallas import tpu as pltpu
from jax.sharding import PartitionSpec as P

MESH = pl.DeviceIdType.MESH
TOTAL_ROWS = 576
GRAD_ROWS = 288
ORDER = -1
DEEP_TYPE = jnp.float32
C = 64
COLS = 16
LAT = 384
SLOTS = COLS + 4
gelu_coef = 0.7978845608
F32 = jnp.float32
BF16 = jnp.bfloat16
NT = (((1,), (1,)), ((), ()))


def loop(start, stop, fn):
    def step(k, carry):
        fn(k)
        return carry

    lax.fori_loop(start, stop, step, 0)


class Grid:
    def __init__(self, dp_size, lon_size):
        self.high = 2 if lon_size == 32 else 1
        self.deep = lon_size // (2 * self.high)
        self.wide = dp_size // 2
        self.tall = 2 * self.high
        self.plane = 2 * self.wide * self.tall
        self.rows = TOTAL_ROWS // self.plane

    def place(self):
        dp = lax.axis_index("dp")
        lon = lax.axis_index("lon")
        x = lax.rem(dp, self.wide)
        y = lax.div(lon, 2 * self.deep) * 2 + lax.div(dp, self.wide)
        z = lax.rem(lax.div(lon, 2), self.deep)
        return x, y, z, lax.rem(lon, 2)

    def device(self, x, y, z, core):
        return (lax.rem(y, 2) * self.wide + x, (lax.div(y, 2) * self.deep + z) * 2 + core)

    def member(self, m, z):
        x = lax.rem(lax.div(m, self.tall), self.wide)
        return self.device(x, lax.rem(m, self.tall), z, lax.div(m, self.wide * self.tall))

    def own(self):
        x, y, z, core = self.place()
        return (core * self.wide + x) * self.tall + y, z

    def greet(self, barrier):
        m, z = self.own()

        def signal(device):
            pl.semaphore_signal(barrier, inc=1, device_id=device, device_id_type=MESH)

        loop(1, self.plane, lambda k: signal(self.member(lax.rem(m + k, self.plane), z)))
        loop(1, self.deep, lambda k: signal(self.member(m, lax.rem(z + k, self.deep))))
        return self.plane + self.deep - 2


def send(src, dst, send_sem, recv_sem, device):
    return pltpu.make_async_remote_copy(
        src_ref=src, dst_ref=dst, send_sem=send_sem, recv_sem=recv_sem, device_id=device, device_id_type=MESH)


class Reduction:
    def __init__(self, grid, factor, out, parts, zparts, whole, plane_sem, deep_sem, gather_sem):
        self.grid, self.factor = grid, factor
        self.out, self.parts, self.zparts, self.whole = out, parts, zparts, whole
        self.plane_sem, self.deep_sem, self.gather_sem = plane_sem, deep_sem, gather_sem
        self.m, self.z = grid.own()

    def offsets(self):
        found = []
        for core in range(2):
            for x in range(self.grid.wide):
                for y in range(self.grid.tall):
                    far = min(x, self.grid.wide - x) + min(y, self.grid.tall - y)
                    found.append((far, core, x, y))
        found = [item[1:] for item in sorted(found, key=lambda item: ORDER * item[0])]
        return [item for item in found if item != (0, 0, 0)]

    def plane_copies(self, arrival, source, target, sem):
        grid = self.grid
        x, y, z, core = grid.place()
        xs = [lax.rem(x + k, grid.wide) for k in range(grid.wide)]
        ys = [lax.rem(y + k, grid.tall) for k in range(grid.tall)]
        cores = [core, 1 - core]
        dps = [[lax.rem(v, 2) * grid.wide + u for v in ys] for u in xs]
        lons = [[(lax.div(v, 2) * grid.deep + z) * 2 + c for v in ys] for c in cores]
        copies = []
        for c, u, v in self.offsets():
            peer = (cores[c] * grid.wide + xs[u]) * grid.tall + ys[v]
            slot = peer if arrival else self.m
            copies.append(send(source(peer), target(slot), sem.at[0], sem.at[1], (dps[u][v], lons[c][v])))
        return copies

    def scatter(self, arrival=False):
        return self.plane_copies(arrival, lambda peer: self.out.at[peer], lambda slot: self.parts.at[slot], self.plane_sem)

    def gather(self, arrival=False):
        return self.plane_copies(arrival, lambda peer: self.whole.at[self.m], lambda slot: self.whole.at[slot], self.gather_sem)

    def across(self, k, arrival=False):
        peer = lax.rem(self.z + k, self.grid.deep)
        slot = peer if arrival else self.z
        return send(self.zparts.at[self.z], self.zparts.at[slot], self.deep_sem.at[0], self.deep_sem.at[1],
                    self.grid.member(self.m, peer))

    def every(self, buffer, sem):
        block = buffer.at[pl.ds(0, self.grid.plane - 1)]
        x, y, z, core = self.grid.place()
        return send(block, block, sem.at[0], sem.at[1], self.grid.device(x, y, z, 1 - core))

    def every_deep(self):
        block = self.zparts.at[pl.ds(0, self.grid.deep - 1)]
        x, y, z, core = self.grid.place()
        return send(block, block, self.deep_sem.at[0], self.deep_sem.at[1], self.grid.device(x, y, z, 1 - core))

    def pack(self, flat, index):
        rows, half = self.grid.rows, self.grid.plane // 2
        for g in range(index * half, (index + 1) * half):
            self.out[g] = flat[g * rows:(g + 1) * rows, :].astype(BF16)

    def start(self):
        self.scatters = self.scatter()
        for copy in self.scatters:
            copy.start()
        self.parts[self.m] = self.out[self.m]

    def after_plane(self):
        self.every(self.parts, self.plane_sem).wait_recv()
        total = self.parts[0].astype(F32)
        for g in range(1, self.grid.plane):
            total = total + self.parts[g].astype(F32)
        self.zparts[self.z] = total.astype(self.zparts.dtype)
        loop(1, self.grid.deep, lambda k: self.across(k).start())

    def after_deep(self):
        self.every_deep().wait_recv()
        total = self.zparts[0].astype(F32)
        for g in range(1, self.grid.deep):
            total = total + self.zparts[g].astype(F32)
        self.whole[self.m] = (total * self.factor).astype(BF16)
        self.gathers = self.gather()
        for copy in self.gathers:
            copy.start()

    def drain(self):
        self.every(self.out, self.plane_sem).wait_send()
        self.every_deep().wait_send()

    def finish(self):
        self.every(self.whole, self.gather_sem).wait_recv()
        self.every(self.whole, self.gather_sem).wait_send()


def net_scratch(grid):
    block = (grid.rows, 128)
    return [
        pltpu.VMEM((grid.plane,) + block, BF16),
        pltpu.VMEM((grid.plane,) + block, BF16),
        pltpu.VMEM((grid.deep,) + block, DEEP_TYPE),
        pltpu.VMEM((grid.plane,) + block, BF16),
        pltpu.SemaphoreType.DMA((2,)),
        pltpu.SemaphoreType.DMA((2,)),
        pltpu.SemaphoreType.DMA((2,)),
    ]


def moved_rows(x):
    lane = lax.broadcasted_iota(jnp.int32, x.shape, 1)
    zero = jnp.zeros_like(x)
    right = jnp.where(lane == 0, zero, pltpu.roll(x, 1, 1))
    left = jnp.where(lane == LAT - 1, zero, pltpu.roll(x, LAT - 1, 1))
    return jnp.concatenate([right, x, left], axis=0)


def dot(a, b):
    return jnp.dot(a, b, preferred_element_type=F32)


def adjoint_taps(k_ref, p):
    row = lax.broadcasted_iota(jnp.int32, (C, C), 0)
    col = lax.broadcasted_iota(jnp.int32, (C, C), 1)
    one = jnp.where(row == col, 1.0, 0.0).astype(BF16)
    stacked = jnp.concatenate([k_ref[p, 2], k_ref[p, 1], k_ref[p, 0]], axis=0)
    return lax.dot_general(one, stacked, NT, preferred_element_type=F32).astype(BF16)


def step_kernel(grid, factor, f_any, t_any, k1_any, k2_any, m_any, out_ref, g_ref,
                f_ref, t_ref, k1_ref, k2_ref, m_ref,
                ft, tt, ts, f3, y, z, hid, d, ds, fg, dh, taps, near, far, acc, flat,
                load_sem, halo_send, halo_recv, outer_sem, *net):
    loads = [pltpu.make_async_copy(source, target, load_sem.at[n]) for n, (source, target) in enumerate(
        ((f_any, f_ref), (t_any, t_ref), (k1_any, k1_ref), (k2_any, k2_ref), (m_any, m_ref)))]
    for load in loads:
        load.start()
    dp, lon = lax.axis_index("dp"), lax.axis_index("lon")
    lon_size = lax.axis_size("lon")
    right = (dp, lax.rem(lon + 1, lon_size))
    left = (dp, lax.rem(lon + lon_size - 1, lon_size))
    barrier = pltpu.get_barrier_semaphore()
    for peer in (left, right):
        pl.semaphore_signal(barrier, inc=1, device_id=peer, device_id_type=MESH)
    greeted = 2 + grid.greet(barrier)

    def turner(source, target):
        def turn(k):
            rows = pl.ds(k * 16, 16)
            target[2:2 + COLS, rows, :] = jnp.swapaxes(source[rows], 0, 1)
        return turn

    copies = []
    for index, (source, ref) in enumerate(((f_ref, ft), (t_ref, tt))):
        loads[index].wait()
        for k in range(C // 16):
            turner(source, ref)(k)
        pair = [send(ref.at[COLS + 1], ref.at[1],
                     halo_send.at[2 * index], halo_recv.at[2 * index], right),
                send(ref.at[2], ref.at[COLS + 2],
                     halo_send.at[2 * index + 1], halo_recv.at[2 * index + 1], left)]
        copies += pair
    pl.semaphore_wait(barrier, greeted)
    for copy in copies:
        copy.start()

    for load in loads[2:]:
        load.wait()
    for p in range(3):
        taps[p * C:(p + 1) * C, :] = jnp.concatenate([k1_ref[p, 0], k1_ref[p, 1], k1_ref[p, 2]], axis=1)
    for index, k_ref in enumerate((k1_ref, k2_ref)):
        far[index] = jnp.concatenate([adjoint_taps(k_ref, 0), adjoint_taps(k_ref, 2)], axis=0)
        near[index] = adjoint_taps(k_ref, 1)
    metric = m_ref[...].reshape(1, LAT)

    def adjoint_block(index, slots, plain, scaled):
        p3 = jnp.concatenate([moved_rows(v) for v in plain], axis=1)
        s3 = jnp.concatenate([moved_rows(v) for v in scaled], axis=1)
        zn = dot(near[index], p3)
        zf = dot(far[index], s3)
        for n, s in enumerate(slots):
            z[s, :2 * C] = zf[:, n * LAT:(n + 1) * LAT]
            z[s, 2 * C:] = zn[:, n * LAT:(n + 1) * LAT]

    def forward_block(slots):
        rows = [moved_rows(ft[s]) for s in slots]
        for n, s in enumerate(slots):
            f3[s] = rows[n]
        yb = dot(taps[...], jnp.concatenate(rows, axis=1))
        for n, s in enumerate(slots):
            y[s] = yb[:, n * LAT:(n + 1) * LAT]

    def reverse_block(slots):
        plain = [tt[s] for s in slots]
        scaled = [(v.astype(F32) * metric).astype(BF16) for v in plain]
        for n, s in enumerate(slots):
            ts[s] = scaled[n]
        adjoint_block(1, slots, plain, scaled)

    def first_block(slots):
        forward_block(slots)
        reverse_block(slots)

    def adjoint_sum(s):
        return z[s, 2 * C:] + z[s - 1, C:2 * C] + z[s + 1, :C]

    def middle(s):
        u = y[s, C:2 * C] + metric * (y[s - 1, :C] + y[s + 1, 2 * C:])
        square = u * u
        inner = jnp.tanh(gelu_coef * (u + 0.044715 * square * u))
        half = 0.5 * (1.0 + inner)
        slope = half + (0.5 * gelu_coef) * u * (1.0 - inner * inner) * (1.0 + 3.0 * 0.044715 * square)
        hid[s] = (u * half).astype(BF16)
        delta = (adjoint_sum(s) * slope).astype(BF16)
        d[s] = delta
        ds[s] = (delta.astype(F32) * metric).astype(BF16)

    def middle_two(s):
        middle(s)
        middle(s + 1)

    def trio(plain, scaled, s):
        return jnp.concatenate([scaled[s + 1], plain[s], scaled[s - 1]], axis=0)

    def second_term(slots):
        h3 = jnp.concatenate([moved_rows(hid[s]) for s in slots], axis=1)
        e3 = jnp.concatenate([trio(tt, ts, s) for s in slots], axis=1)
        acc[1] += lax.dot_general(e3, h3, NT, preferred_element_type=F32)

    def first_term(slots):
        v3 = jnp.concatenate([f3[s] for s in slots], axis=1)
        d3 = jnp.concatenate([trio(d, ds, s) for s in slots], axis=1)
        acc[0] += lax.dot_general(d3, v3, NT, preferred_element_type=F32)

    def terms(b):
        second_term([3 + 7 * b + n for n in range(7)])
        first_term([4 + 6 * b + n for n in range(6)])

    acc[...] = jnp.zeros_like(acc)
    for s in (0, 1, COLS + 2, COLS + 3):
        d[s] = jnp.zeros((C, LAT), BF16)
        ds[s] = jnp.zeros((C, LAT), BF16)
    for b in range(2):
        first_block([2 + 8 * b + n for n in range(8)])
    for b in range(7):
        middle(3 + b)
    second_term([3 + n for n in range(7)])
    for b in range(7, 14):
        middle(3 + b)
    second_term([10 + n for n in range(7)])
    first_term([4 + n for n in range(6)])
    first_term([10 + n for n in range(6)])
    reduction = Reduction(grid, factor, *net)

    def pack(index):
        base = index * GRAD_ROWS
        flat[base:base + 192, :] = acc[index, :, :128]
        flat[base + 192:base + GRAD_ROWS, :] = jnp.concatenate([acc[index, :96, 128:], acc[index, 96:, 128:]], axis=1)
        reduction.pack(flat, index)

    edges = [1, COLS + 2]
    for copy in copies[:2]:
        copy.wait_recv()
    forward_block(edges)
    for copy in copies[2:]:
        copy.wait_recv()
    reverse_block(edges)
    middle(2)
    middle(COLS + 1)
    second_term([2, COLS + 1])
    pack(1)
    first_term([1, 2, 3, COLS, COLS + 1, COLS + 2])
    pack(0)
    reduction.start()
    outer = [send(d.at[COLS + 1], dh.at[0], outer_sem.at[0], outer_sem.at[2], right),
             send(d.at[2], dh.at[1], outer_sem.at[1], outer_sem.at[3], left)]
    for copy in outer:
        copy.start()

    def last_block(slots):
        adjoint_block(0, slots, [d[s] for s in slots], [ds[s] for s in slots])

    def finish(s):
        fg[s - 2] = (tt[s].astype(F32) + adjoint_sum(s)).astype(BF16)

    def finish_two(b):
        finish(3 + 2 * b)
        finish(4 + 2 * b)

    def turn_back(k):
        part = pl.ds(pl.multiple_of(k * 16, 16), 16)
        out_ref[part] = jnp.swapaxes(fg[:, part, :], 0, 1)

    loop(0, 4, lambda b: last_block([2 + 4 * b + n for n in range(4)]))
    loop(0, COLS // 2 - 1, finish_two)
    reduction.after_plane()
    for copy in copies:
        copy.wait_send()
    for n, s in enumerate(edges):
        outer[n].wait_recv()
        d[s] = dh[n]
        ds[s] = (dh[n].astype(F32) * metric).astype(BF16)
    last_block(edges)
    finish(2)
    finish(COLS + 1)
    loop(0, C // 16, turn_back)
    reduction.after_deep()
    for copy in outer:
        copy.wait_send()
    reduction.drain()
    reduction.finish()
    g_ref[...] = reduction.whole[...]


def format_kernel(grid, x_ref, g_ref, out_ref, g1_ref, g2_ref, flat, sem):
    copy = pltpu.make_async_copy(x_ref, out_ref, sem)
    copy.start()
    rows = grid.rows
    for g in range(TOTAL_ROWS // rows):
        flat[g * rows:(g + 1) * rows, :] = g_ref[g].astype(F32)
    for index, ref in enumerate((g1_ref, g2_ref)):
        for p in range(3):
            base = index * GRAD_ROWS + p * C
            pair = flat[base:base + C, :]
            ref[p, 0] = pair[:, :C].astype(BF16)
            ref[p, 1] = pair[:, C:].astype(BF16)
        side = flat[index * GRAD_ROWS + 192:(index + 1) * GRAD_ROWS, :]
        rest = jnp.concatenate([side[:, :C], side[:, C:]], axis=0)
        for p in range(3):
            ref[p, 2] = rest[p * C:(p + 1) * C].astype(BF16)
    copy.wait()


def per_device(fields, cotangent, kernel_first, kernel_second, metric):
    dp_size, lon_size = lax.axis_size("dp"), lax.axis_size("lon")
    grid = Grid(dp_size, lon_size)
    factor = 1.0 / (float(dp_size) * float(COLS * lon_size) * float(LAT)) ** 0.5
    vmem = pl.BlockSpec(memory_space=pltpu.VMEM)
    anywhere = pl.BlockSpec(memory_space=pl.ANY)
    taps = (3, 3, C, C)
    column = pltpu.VMEM((SLOTS, C, LAT), BF16)
    turned, packed = pl.pallas_call(
        functools.partial(step_kernel, grid, factor),
        out_shape=(
            pltpu.VMEM((C, COLS, LAT), BF16),
            pltpu.VMEM((grid.plane, grid.rows, 128), BF16),
        ),
        in_specs=[anywhere] * 5,
        out_specs=(vmem, vmem),
        scratch_shapes=[
            pltpu.VMEM((C, COLS, LAT), BF16),
            pltpu.VMEM((C, COLS, LAT), BF16),
            pltpu.VMEM(taps, BF16),
            pltpu.VMEM(taps, BF16),
            pltpu.VMEM((LAT,), F32),
            column,
            column,
            column,
            pltpu.VMEM((SLOTS, 3 * C, LAT), BF16),
            pltpu.VMEM((SLOTS, 3 * C, LAT), F32),
            pltpu.VMEM((SLOTS, 3 * C, LAT), F32),
            column,
            column,
            column,
            pltpu.VMEM((COLS, C, LAT), BF16),
            pltpu.VMEM((2, C, LAT), BF16),
            pltpu.VMEM((3 * C, 3 * C), BF16),
            pltpu.VMEM((2, C, 3 * C), BF16),
            pltpu.VMEM((2, 2 * C, 3 * C), BF16),
            pltpu.VMEM((2, 3 * C, 3 * C), F32),
            pltpu.VMEM((TOTAL_ROWS, 128), F32),
            pltpu.SemaphoreType.DMA((5,)),
            pltpu.SemaphoreType.DMA((4,)),
            pltpu.SemaphoreType.DMA((4,)),
            pltpu.SemaphoreType.DMA((4,)),
        ] + net_scratch(grid),
        compiler_params=pltpu.CompilerParams(
            collective_id=0, has_side_effects=True, vmem_limit_bytes=60 * 2**20),
    )(fields[0], cotangent[0], kernel_first, kernel_second, metric)
    field_grad, first, second = pl.pallas_call(
        functools.partial(format_kernel, grid),
        out_shape=(
            jax.ShapeDtypeStruct((C, COLS, LAT), BF16),
            jax.ShapeDtypeStruct(taps, BF16),
            jax.ShapeDtypeStruct(taps, BF16),
        ),
        in_specs=[vmem, vmem],
        out_specs=(anywhere, vmem, vmem),
        scratch_shapes=[pltpu.VMEM((TOTAL_ROWS, 128), F32), pltpu.SemaphoreType.DMA(())],
        compiler_params=pltpu.CompilerParams(vmem_limit_bytes=16 * 2**20),
    )(turned, packed)
    return field_grad[None], first, second


def solution(mesh):
    placed = (P("dp", None, "lon", None), P("dp", None, "lon", None), P(), P(), P())
    return jax.shard_map(
        per_device,
        mesh=mesh,
        in_specs=placed,
        out_specs=(P("dp", None, "lon", None), P(), P()),
        check_vma=False,
    )
```

```python
import functools
import jax
import jax.numpy as jnp
from jax import lax
from jax.experimental import pallas as pl
from jax.experimental.pallas import tpu as pltpu
from jax.sharding import PartitionSpec as P

MESH = pl.DeviceIdType.MESH
TOTAL_ROWS = 576
GRAD_ROWS = 288
ORDER = -1
DEEP_TYPE = jnp.float32
C = 64
COLS = 16
LAT = 384
SLOTS = COLS + 4
gelu_coef = 0.7978845608
F32 = jnp.float32
BF16 = jnp.bfloat16
NT = (((1,), (1,)), ((), ()))


def loop(start, stop, fn):
    def step(k, carry):
        fn(k)
        return carry

    lax.fori_loop(start, stop, step, 0)


class Grid:
    def __init__(self, dp_size, lon_size):
        self.high = 2 if lon_size == 32 else 1
        self.deep = lon_size // (2 * self.high)
        self.wide = dp_size // 2
        self.tall = 2 * self.high
        self.plane = 2 * self.wide * self.tall
        self.rows = TOTAL_ROWS // self.plane

    def place(self):
        dp = lax.axis_index("dp")
        lon = lax.axis_index("lon")
        x = lax.rem(dp, self.wide)
        y = lax.div(lon, 2 * self.deep) * 2 + lax.div(dp, self.wide)
        z = lax.rem(lax.div(lon, 2), self.deep)
        return x, y, z, lax.rem(lon, 2)

    def device(self, x, y, z, core):
        return (lax.rem(y, 2) * self.wide + x, (lax.div(y, 2) * self.deep + z) * 2 + core)

    def member(self, m, z):
        x = lax.rem(lax.div(m, self.tall), self.wide)
        return self.device(x, lax.rem(m, self.tall), z, lax.div(m, self.wide * self.tall))

    def own(self):
        x, y, z, core = self.place()
        return (core * self.wide + x) * self.tall + y, z

    def greet(self, barrier, left, right):
        x, y, z, core = self.place()
        xs = [lax.rem(x + k, self.wide) for k in range(self.wide)]
        ys = [lax.rem(y + k, self.tall) for k in range(self.tall)]
        cores = [core, 1 - core]
        dps = [[lax.rem(v, 2) * self.wide + u for v in ys] for u in xs]
        bases = [lax.div(v, 2) * self.deep for v in ys]
        targets = []
        for c in range(2):
            for u in range(self.wide):
                for v in range(self.tall):
                    far = min(u, self.wide - u) + min(v, self.tall - v)
                    targets.append((far, (dps[u][v], (bases[v] + z) * 2 + cores[c]), c or u or v))
        for k in range(1, self.deep):
            targets.append((min(k, self.deep - k), (dps[0][0], (bases[0] + lax.rem(z + k, self.deep)) * 2 + core), True))
        targets += [(1.5, left, True), (1.5, right, True)]
        targets = [item for item in sorted(targets, key=lambda item: -item[0]) if item[2]]
        for item in targets:
            pl.semaphore_signal(barrier, inc=1, device_id=item[1], device_id_type=MESH)
        return len(targets)


def send(src, dst, send_sem, recv_sem, device):
    return pltpu.make_async_remote_copy(
        src_ref=src, dst_ref=dst, send_sem=send_sem, recv_sem=recv_sem, device_id=device, device_id_type=MESH)


class Reduction:
    def __init__(self, grid, factor, out, parts, zparts, whole, plane_sem, deep_sem, gather_sem):
        self.grid, self.factor = grid, factor
        self.out, self.parts, self.zparts, self.whole = out, parts, zparts, whole
        self.plane_sem, self.deep_sem, self.gather_sem = plane_sem, deep_sem, gather_sem
        self.m, self.z = grid.own()

    def offsets(self):
        found = []
        for core in range(2):
            for x in range(self.grid.wide):
                for y in range(self.grid.tall):
                    far = min(x, self.grid.wide - x) + min(y, self.grid.tall - y)
                    found.append((far, core, x, y))
        found = [item[1:] for item in sorted(found, key=lambda item: ORDER * item[0])]
        return [item for item in found if item != (0, 0, 0)]

    def plane_copies(self, arrival, source, target, sem, goal=None):
        grid = self.grid
        x, y, z, core = grid.place()
        xs = [lax.rem(x + k, grid.wide) for k in range(grid.wide)]
        ys = [lax.rem(y + k, grid.tall) for k in range(grid.tall)]
        cores = [core, 1 - core] if goal is None else [goal]
        dps = [[lax.rem(v, 2) * grid.wide + u for v in ys] for u in xs]
        lons = [[(lax.div(v, 2) * grid.deep + z) * 2 + c for v in ys] for c in cores]
        copies = []
        for c, u, v in self.offsets():
            if goal is not None and (c or not (u or v)):
                continue
            peer = (cores[c] * grid.wide + xs[u]) * grid.tall + ys[v]
            slot = peer if arrival else self.m
            copies.append(send(source(peer), target(slot), sem.at[0], sem.at[1], (dps[u][v], lons[c][v])))
        return copies

    def scatter(self, goal):
        for copy in self.plane_copies(False, lambda peer: self.out.at[peer], lambda slot: self.parts.at[slot], self.plane_sem, goal):
            copy.start()

    def scatter_partner(self):
        x, y, z, core = self.grid.place()
        half = self.grid.plane // 2
        peer = self.m + half - 2 * half * core
        send(self.out.at[peer], self.parts.at[self.m], self.plane_sem.at[0], self.plane_sem.at[1],
             self.grid.device(x, y, z, 1 - core)).start()
        self.parts[self.m] = self.out[self.m]

    def gather(self, arrival=False):
        return self.plane_copies(arrival, lambda peer: self.whole.at[self.m], lambda slot: self.whole.at[slot], self.gather_sem)

    def across(self, k, arrival=False):
        peer = lax.rem(self.z + k, self.grid.deep)
        slot = peer if arrival else self.z
        return send(self.zparts.at[self.z], self.zparts.at[slot], self.deep_sem.at[0], self.deep_sem.at[1],
                    self.grid.member(self.m, peer))

    def every(self, buffer, sem):
        block = buffer.at[pl.ds(0, self.grid.plane - 1)]
        x, y, z, core = self.grid.place()
        return send(block, block, sem.at[0], sem.at[1], self.grid.device(x, y, z, 1 - core))

    def every_deep(self):
        block = self.zparts.at[pl.ds(0, self.grid.deep - 1)]
        x, y, z, core = self.grid.place()
        return send(block, block, self.deep_sem.at[0], self.deep_sem.at[1], self.grid.device(x, y, z, 1 - core))

    def pack(self, flat, index):
        rows, half = self.grid.rows, self.grid.plane // 2
        for g in range(index * half, (index + 1) * half):
            self.out[g] = flat[g * rows:(g + 1) * rows, :].astype(BF16)

    def after_plane(self):
        self.every(self.parts, self.plane_sem).wait_recv()
        total = self.parts[0].astype(F32)
        for g in range(1, self.grid.plane):
            total = total + self.parts[g].astype(F32)
        self.zparts[self.z] = total.astype(self.zparts.dtype)
        loop(1, self.grid.deep, lambda k: self.across(k).start())

    def after_deep(self):
        self.every_deep().wait_recv()
        total = self.zparts[0].astype(F32)
        for g in range(1, self.grid.deep):
            total = total + self.zparts[g].astype(F32)
        self.whole[self.m] = (total * self.factor).astype(BF16)
        self.gathers = self.gather()
        for copy in self.gathers:
            copy.start()

    def drain(self):
        self.every(self.out, self.plane_sem).wait_send()
        self.every_deep().wait_send()

    def finish(self):
        self.every(self.whole, self.gather_sem).wait_recv()
        self.every(self.whole, self.gather_sem).wait_send()


def net_scratch(grid):
    block = (grid.rows, 128)
    return [
        pltpu.VMEM((grid.plane,) + block, BF16),
        pltpu.VMEM((grid.plane,) + block, BF16),
        pltpu.VMEM((grid.deep,) + block, DEEP_TYPE),
        pltpu.VMEM((grid.plane,) + block, BF16),
        pltpu.SemaphoreType.DMA((2,)),
        pltpu.SemaphoreType.DMA((2,)),
        pltpu.SemaphoreType.DMA((2,)),
    ]


def moved_rows(x):
    lane = lax.broadcasted_iota(jnp.int32, x.shape, 1)
    zero = jnp.zeros_like(x)
    right = jnp.where(lane == 0, zero, pltpu.roll(x, 1, 1))
    left = jnp.where(lane == LAT - 1, zero, pltpu.roll(x, LAT - 1, 1))
    return jnp.concatenate([right, x, left], axis=0)


def dot(a, b):
    return jnp.dot(a, b, preferred_element_type=F32)


def adjoint_taps(k_ref, p):
    row = lax.broadcasted_iota(jnp.int32, (C, C), 0)
    col = lax.broadcasted_iota(jnp.int32, (C, C), 1)
    one = jnp.where(row == col, 1.0, 0.0).astype(BF16)
    stacked = jnp.concatenate([k_ref[p, 2], k_ref[p, 1], k_ref[p, 0]], axis=0)
    return lax.dot_general(one, stacked, NT, preferred_element_type=F32).astype(BF16)


def step_kernel(grid, factor, f_any, t_any, k1_any, k2_any, m_any, out_ref, g_ref,
                f_ref, t_ref, k1_ref, k2_ref, m_ref,
                ft, tt, ts, f3, y, z, hid, d, ds, fg, dh, taps, near, far, acc, flat,
                load_sem, halo_send, halo_recv, outer_sem, *net):
    loads = [pltpu.make_async_copy(source, target, load_sem.at[n]) for n, (source, target) in enumerate(
        ((f_any, f_ref), (t_any, t_ref), (k1_any, k1_ref), (k2_any, k2_ref), (m_any, m_ref)))]
    for load in loads:
        load.start()
    dp, lon = lax.axis_index("dp"), lax.axis_index("lon")
    lon_size = lax.axis_size("lon")
    right = (dp, lax.rem(lon + 1, lon_size))
    left = (dp, lax.rem(lon + lon_size - 1, lon_size))
    barrier = pltpu.get_barrier_semaphore()
    greeted = grid.greet(barrier, left, right)

    def turner(source, target):
        def turn(k):
            rows = pl.ds(k * 16, 16)
            target[2:2 + COLS, rows, :] = jnp.swapaxes(source[rows], 0, 1)
        return turn

    copies = []
    for index, (source, ref) in enumerate(((f_ref, ft), (t_ref, tt))):
        loads[index].wait()
        for k in range(C // 16):
            turner(source, ref)(k)
        pair = [send(ref.at[COLS + 1], ref.at[1],
                     halo_send.at[2 * index], halo_recv.at[2 * index], right),
                send(ref.at[2], ref.at[COLS + 2],
                     halo_send.at[2 * index + 1], halo_recv.at[2 * index + 1], left)]
        copies += pair
    pl.semaphore_wait(barrier, greeted)
    for copy in copies:
        copy.start()

    for load in loads[2:]:
        load.wait()
    for p in range(3):
        taps[p * C:(p + 1) * C, :] = jnp.concatenate([k1_ref[p, 0], k1_ref[p, 1], k1_ref[p, 2]], axis=1)
    for index, k_ref in enumerate((k1_ref, k2_ref)):
        far[index] = jnp.concatenate([adjoint_taps(k_ref, 0), adjoint_taps(k_ref, 2)], axis=0)
        near[index] = adjoint_taps(k_ref, 1)
    metric = m_ref[...].reshape(1, LAT)

    def adjoint_block(index, slots, plain, scaled):
        p3 = jnp.concatenate([moved_rows(v) for v in plain], axis=1)
        s3 = jnp.concatenate([moved_rows(v) for v in scaled], axis=1)
        zn = dot(near[index], p3)
        zf = dot(far[index], s3)
        for n, s in enumerate(slots):
            z[s, :2 * C] = zf[:, n * LAT:(n + 1) * LAT]
            z[s, 2 * C:] = zn[:, n * LAT:(n + 1) * LAT]

    def forward_block(slots):
        rows = [moved_rows(ft[s]) for s in slots]
        for n, s in enumerate(slots):
            f3[s] = rows[n]
        yb = dot(taps[...], jnp.concatenate(rows, axis=1))
        for n, s in enumerate(slots):
            y[s] = yb[:, n * LAT:(n + 1) * LAT]

    def reverse_block(slots):
        plain = [tt[s] for s in slots]
        scaled = [(v.astype(F32) * metric).astype(BF16) for v in plain]
        for n, s in enumerate(slots):
            ts[s] = scaled[n]
        adjoint_block(1, slots, plain, scaled)

    def first_block(slots):
        forward_block(slots)
        reverse_block(slots)

    def adjoint_sum(s):
        return z[s, 2 * C:] + z[s - 1, C:2 * C] + z[s + 1, :C]

    def middle(s):
        u = y[s, C:2 * C] + metric * (y[s - 1, :C] + y[s + 1, 2 * C:])
        square = u * u
        inner = jnp.tanh(gelu_coef * (u + 0.044715 * square * u))
        half = 0.5 * (1.0 + inner)
        slope = half + (0.5 * gelu_coef) * u * (1.0 - inner * inner) * (1.0 + 3.0 * 0.044715 * square)
        hid[s] = (u * half).astype(BF16)
        delta = (adjoint_sum(s) * slope).astype(BF16)
        d[s] = delta
        ds[s] = (delta.astype(F32) * metric).astype(BF16)

    def middle_two(s):
        middle(s)
        middle(s + 1)

    def trio(plain, scaled, s):
        return jnp.concatenate([scaled[s + 1], plain[s], scaled[s - 1]], axis=0)

    def second_term(slots):
        h3 = jnp.concatenate([moved_rows(hid[s]) for s in slots], axis=1)
        e3 = jnp.concatenate([trio(tt, ts, s) for s in slots], axis=1)
        acc[1] += lax.dot_general(e3, h3, NT, preferred_element_type=F32)

    def first_term(slots):
        v3 = jnp.concatenate([f3[s] for s in slots], axis=1)
        d3 = jnp.concatenate([trio(d, ds, s) for s in slots], axis=1)
        acc[0] += lax.dot_general(d3, v3, NT, preferred_element_type=F32)

    def terms(b):
        second_term([3 + 7 * b + n for n in range(7)])
        first_term([4 + 6 * b + n for n in range(6)])

    acc[...] = jnp.zeros_like(acc)
    for s in (0, 1, COLS + 2, COLS + 3):
        d[s] = jnp.zeros((C, LAT), BF16)
        ds[s] = jnp.zeros((C, LAT), BF16)
    for b in range(2):
        first_block([2 + 8 * b + n for n in range(8)])
    for b in range(7):
        middle(3 + b)
    second_term([3 + n for n in range(7)])
    for b in range(7, 14):
        middle(3 + b)
    second_term([10 + n for n in range(7)])
    reduction = Reduction(grid, factor, *net)

    def pack(index):
        base = index * GRAD_ROWS
        flat[base:base + 192, :] = acc[index, :, :128]
        flat[base + 192:base + GRAD_ROWS, :] = jnp.concatenate([acc[index, :96, 128:], acc[index, 96:, 128:]], axis=1)
        reduction.pack(flat, index)

    edges = [1, COLS + 2]
    for copy in copies[:2]:
        copy.wait_recv()
    forward_block(edges)
    for copy in copies[2:]:
        copy.wait_recv()
    reverse_block(edges)
    middle(2)
    middle(COLS + 1)
    second_term([2, COLS + 1])
    pack(1)
    reduction.scatter(1)
    first_term([1 + n for n in range(9)])
    first_term([10 + n for n in range(9)])
    pack(0)
    reduction.scatter(0)
    reduction.scatter_partner()
    outer = [send(d.at[COLS + 1], dh.at[0], outer_sem.at[0], outer_sem.at[2], right),
             send(d.at[2], dh.at[1], outer_sem.at[1], outer_sem.at[3], left)]
    for copy in outer:
        copy.start()

    def last_block(slots):
        adjoint_block(0, slots, [d[s] for s in slots], [ds[s] for s in slots])

    def finish(s):
        fg[s - 2] = (tt[s].astype(F32) + adjoint_sum(s)).astype(BF16)

    def finish_two(b):
        finish(3 + 2 * b)
        finish(4 + 2 * b)

    def turn_back(k):
        part = pl.ds(pl.multiple_of(k * 16, 16), 16)
        out_ref[part] = jnp.swapaxes(fg[:, part, :], 0, 1)

    loop(0, 4, lambda b: last_block([2 + 4 * b + n for n in range(4)]))
    loop(0, COLS // 2 - 1, finish_two)
    reduction.after_plane()
    for copy in copies:
        copy.wait_send()
    for n, s in enumerate(edges):
        outer[n].wait_recv()
        d[s] = dh[n]
        ds[s] = (dh[n].astype(F32) * metric).astype(BF16)
    last_block(edges)
    finish(2)
    finish(COLS + 1)
    loop(0, C // 16, turn_back)
    reduction.after_deep()
    for copy in outer:
        copy.wait_send()
    reduction.drain()
    reduction.finish()
    g_ref[...] = reduction.whole[...]


def format_kernel(grid, x_ref, g_ref, out_ref, g1_ref, g2_ref, flat, sem):
    copy = pltpu.make_async_copy(x_ref, out_ref, sem)
    copy.start()
    rows = grid.rows
    for g in range(TOTAL_ROWS // rows):
        flat[g * rows:(g + 1) * rows, :] = g_ref[g].astype(F32)
    for index, ref in enumerate((g1_ref, g2_ref)):
        for p in range(3):
            base = index * GRAD_ROWS + p * C
            pair = flat[base:base + C, :]
            ref[p, 0] = pair[:, :C].astype(BF16)
            ref[p, 1] = pair[:, C:].astype(BF16)
        side = flat[index * GRAD_ROWS + 192:(index + 1) * GRAD_ROWS, :]
        rest = jnp.concatenate([side[:, :C], side[:, C:]], axis=0)
        for p in range(3):
            ref[p, 2] = rest[p * C:(p + 1) * C].astype(BF16)
    copy.wait()


def per_device(fields, cotangent, kernel_first, kernel_second, metric):
    dp_size, lon_size = lax.axis_size("dp"), lax.axis_size("lon")
    grid = Grid(dp_size, lon_size)
    factor = 1.0 / (float(dp_size) * float(COLS * lon_size) * float(LAT)) ** 0.5
    vmem = pl.BlockSpec(memory_space=pltpu.VMEM)
    anywhere = pl.BlockSpec(memory_space=pl.ANY)
    taps = (3, 3, C, C)
    column = pltpu.VMEM((SLOTS, C, LAT), BF16)
    turned, packed = pl.pallas_call(
        functools.partial(step_kernel, grid, factor),
        out_shape=(
            pltpu.VMEM((C, COLS, LAT), BF16),
            pltpu.VMEM((grid.plane, grid.rows, 128), BF16),
        ),
        in_specs=[anywhere] * 5,
        out_specs=(vmem, vmem),
        scratch_shapes=[
            pltpu.VMEM((C, COLS, LAT), BF16),
            pltpu.VMEM((C, COLS, LAT), BF16),
            pltpu.VMEM(taps, BF16),
            pltpu.VMEM(taps, BF16),
            pltpu.VMEM((LAT,), F32),
            column,
            column,
            column,
            pltpu.VMEM((SLOTS, 3 * C, LAT), BF16),
            pltpu.VMEM((SLOTS, 3 * C, LAT), F32),
            pltpu.VMEM((SLOTS, 3 * C, LAT), F32),
            column,
            column,
            column,
            pltpu.VMEM((COLS, C, LAT), BF16),
            pltpu.VMEM((2, C, LAT), BF16),
            pltpu.VMEM((3 * C, 3 * C), BF16),
            pltpu.VMEM((2, C, 3 * C), BF16),
            pltpu.VMEM((2, 2 * C, 3 * C), BF16),
            pltpu.VMEM((2, 3 * C, 3 * C), F32),
            pltpu.VMEM((TOTAL_ROWS, 128), F32),
            pltpu.SemaphoreType.DMA((5,)),
            pltpu.SemaphoreType.DMA((4,)),
            pltpu.SemaphoreType.DMA((4,)),
            pltpu.SemaphoreType.DMA((4,)),
        ] + net_scratch(grid),
        compiler_params=pltpu.CompilerParams(
            collective_id=0, has_side_effects=True, vmem_limit_bytes=60 * 2**20),
    )(fields[0], cotangent[0], kernel_first, kernel_second, metric)
    field_grad, first, second = pl.pallas_call(
        functools.partial(format_kernel, grid),
        out_shape=(
            jax.ShapeDtypeStruct((C, COLS, LAT), BF16),
            jax.ShapeDtypeStruct(taps, BF16),
            jax.ShapeDtypeStruct(taps, BF16),
        ),
        in_specs=[vmem, vmem],
        out_specs=(anywhere, vmem, vmem),
        scratch_shapes=[pltpu.VMEM((TOTAL_ROWS, 128), F32), pltpu.SemaphoreType.DMA(())],
        compiler_params=pltpu.CompilerParams(vmem_limit_bytes=16 * 2**20),
    )(turned, packed)
    return field_grad[None], first, second


def solution(mesh):
    placed = (P("dp", None, "lon", None), P("dp", None, "lon", None), P(), P(), P())
    return jax.shard_map(
        per_device,
        mesh=mesh,
        in_specs=placed,
        out_specs=(P("dp", None, "lon", None), P(), P()),
        check_vma=False,
    )
```

```python
import functools
import jax
import jax.numpy as jnp
from jax import lax
from jax.experimental import pallas as pl
from jax.experimental.pallas import tpu as pltpu
from jax.sharding import PartitionSpec as P

MESH = pl.DeviceIdType.MESH
TOTAL_ROWS = 576
GRAD_ROWS = 288
ORDER = -1
DEEP_TYPE = jnp.float32
C = 64
COLS = 16
LAT = 384
SLOTS = COLS + 4
gelu_coef = 0.7978845608
F32 = jnp.float32
BF16 = jnp.bfloat16
NT = (((1,), (1,)), ((), ()))


def loop(start, stop, fn):
    def step(k, carry):
        fn(k)
        return carry

    lax.fori_loop(start, stop, step, 0)


class Grid:
    def __init__(self, dp_size, lon_size):
        self.high = 2 if lon_size == 32 else 1
        self.deep = lon_size // (2 * self.high)
        self.wide = dp_size // 2
        self.tall = 2 * self.high
        self.plane = 2 * self.wide * self.tall
        self.rows = TOTAL_ROWS // self.plane

    def place(self):
        dp = lax.axis_index("dp")
        lon = lax.axis_index("lon")
        x = lax.rem(dp, self.wide)
        y = lax.div(lon, 2 * self.deep) * 2 + lax.div(dp, self.wide)
        z = lax.rem(lax.div(lon, 2), self.deep)
        return x, y, z, lax.rem(lon, 2)

    def device(self, x, y, z, core):
        return (lax.rem(y, 2) * self.wide + x, (lax.div(y, 2) * self.deep + z) * 2 + core)

    def member(self, m, z):
        x = lax.rem(lax.div(m, self.tall), self.wide)
        return self.device(x, lax.rem(m, self.tall), z, lax.div(m, self.wide * self.tall))

    def own(self):
        x, y, z, core = self.place()
        return (core * self.wide + x) * self.tall + y, z

    def greet(self, barrier, left, right):
        x, y, z, core = self.place()
        xs = [lax.rem(x + k, self.wide) for k in range(self.wide)]
        ys = [lax.rem(y + k, self.tall) for k in range(self.tall)]
        cores = [core, 1 - core]
        dps = [[lax.rem(v, 2) * self.wide + u for v in ys] for u in xs]
        bases = [lax.div(v, 2) * self.deep for v in ys]
        targets = []
        for c in range(2):
            for u in range(self.wide):
                for v in range(self.tall):
                    far = min(u, self.wide - u) + min(v, self.tall - v)
                    targets.append((far, (dps[u][v], (bases[v] + z) * 2 + cores[c]), c or u or v))
        for k in range(1, self.deep):
            targets.append((min(k, self.deep - k), (dps[0][0], (bases[0] + lax.rem(z + k, self.deep)) * 2 + core), True))
        targets += [(1.5, left, True), (1.5, right, True)]
        targets = [item for item in sorted(targets, key=lambda item: -item[0]) if item[2]]
        for item in targets:
            pl.semaphore_signal(barrier, inc=1, device_id=item[1], device_id_type=MESH)
        return len(targets)


def send(src, dst, send_sem, recv_sem, device):
    return pltpu.make_async_remote_copy(
        src_ref=src, dst_ref=dst, send_sem=send_sem, recv_sem=recv_sem, device_id=device, device_id_type=MESH)


class Reduction:
    def __init__(self, grid, factor, out, parts, zparts, whole, plane_sem, deep_sem, gather_sem):
        self.grid, self.factor = grid, factor
        self.out, self.parts, self.zparts, self.whole = out, parts, zparts, whole
        self.plane_sem, self.deep_sem, self.gather_sem = plane_sem, deep_sem, gather_sem
        self.m, self.z = grid.own()

    def offsets(self):
        found = []
        for core in range(2):
            for x in range(self.grid.wide):
                for y in range(self.grid.tall):
                    far = min(x, self.grid.wide - x) + min(y, self.grid.tall - y)
                    found.append((far, core, x, y))
        found = [item[1:] for item in sorted(found, key=lambda item: ORDER * item[0])]
        return [item for item in found if item != (0, 0, 0)]

    def plane_copies(self, arrival, source, target, sem, goal=None):
        grid = self.grid
        x, y, z, core = grid.place()
        xs = [lax.rem(x + k, grid.wide) for k in range(grid.wide)]
        ys = [lax.rem(y + k, grid.tall) for k in range(grid.tall)]
        cores = [core, 1 - core] if goal is None else [goal]
        dps = [[lax.rem(v, 2) * grid.wide + u for v in ys] for u in xs]
        lons = [[(lax.div(v, 2) * grid.deep + z) * 2 + c for v in ys] for c in cores]
        copies = []
        for c, u, v in self.offsets():
            if goal is not None and (c or not (u or v)):
                continue
            peer = (cores[c] * grid.wide + xs[u]) * grid.tall + ys[v]
            slot = peer if arrival else self.m
            copies.append(send(source(peer), target(slot), sem.at[0], sem.at[1], (dps[u][v], lons[c][v])))
        return copies

    def scatter(self, goal):
        for copy in self.plane_copies(False, lambda peer: self.out.at[peer], lambda slot: self.parts.at[slot], self.plane_sem, goal):
            copy.start()

    def scatter_partner(self):
        x, y, z, core = self.grid.place()
        half = self.grid.plane // 2
        peer = self.m + half - 2 * half * core
        send(self.out.at[peer], self.parts.at[self.m], self.plane_sem.at[0], self.plane_sem.at[1],
             self.grid.device(x, y, z, 1 - core)).start()
        self.parts[self.m] = self.out[self.m]

    def gather(self, arrival=False):
        return self.plane_copies(arrival, lambda peer: self.whole.at[self.m], lambda slot: self.whole.at[slot], self.gather_sem)

    def across(self, k, arrival=False):
        peer = lax.rem(self.z + k, self.grid.deep)
        slot = peer if arrival else self.z
        return send(self.zparts.at[self.z], self.zparts.at[slot], self.deep_sem.at[0], self.deep_sem.at[1],
                    self.grid.member(self.m, peer))

    def every(self, buffer, sem):
        block = buffer.at[pl.ds(0, self.grid.plane - 1)]
        x, y, z, core = self.grid.place()
        return send(block, block, sem.at[0], sem.at[1], self.grid.device(x, y, z, 1 - core))

    def every_deep(self):
        block = self.zparts.at[pl.ds(0, self.grid.deep - 1)]
        x, y, z, core = self.grid.place()
        return send(block, block, self.deep_sem.at[0], self.deep_sem.at[1], self.grid.device(x, y, z, 1 - core))

    def pack(self, flat, index):
        rows, half = self.grid.rows, self.grid.plane // 2
        for g in range(index * half, (index + 1) * half):
            self.out[g] = flat[g * rows:(g + 1) * rows, :].astype(BF16)

    def after_plane(self):
        self.every(self.parts, self.plane_sem).wait_recv()
        total = self.parts[0].astype(F32)
        for g in range(1, self.grid.plane):
            total = total + self.parts[g].astype(F32)
        self.zparts[self.z] = total.astype(self.zparts.dtype)
        for k in sorted(range(1, self.grid.deep), key=lambda k: -min(k, self.grid.deep - k)):
            self.across(k).start()

    def after_deep(self):
        self.every_deep().wait_recv()
        total = self.zparts[0].astype(F32)
        for g in range(1, self.grid.deep):
            total = total + self.zparts[g].astype(F32)
        self.whole[self.m] = (total * self.factor).astype(BF16)
        self.gathers = self.gather()
        for copy in self.gathers:
            copy.start()

    def drain(self):
        self.every(self.out, self.plane_sem).wait_send()
        self.every_deep().wait_send()

    def finish(self):
        self.every(self.whole, self.gather_sem).wait_recv()
        self.every(self.whole, self.gather_sem).wait_send()


def net_scratch(grid):
    block = (grid.rows, 128)
    return [
        pltpu.VMEM((grid.plane,) + block, BF16),
        pltpu.VMEM((grid.plane,) + block, BF16),
        pltpu.VMEM((grid.deep,) + block, DEEP_TYPE),
        pltpu.VMEM((grid.plane,) + block, BF16),
        pltpu.SemaphoreType.DMA((2,)),
        pltpu.SemaphoreType.DMA((2,)),
        pltpu.SemaphoreType.DMA((2,)),
    ]


def moved_rows(x):
    lane = lax.broadcasted_iota(jnp.int32, x.shape, 1)
    zero = jnp.zeros_like(x)
    right = jnp.where(lane == 0, zero, pltpu.roll(x, 1, 1))
    left = jnp.where(lane == LAT - 1, zero, pltpu.roll(x, LAT - 1, 1))
    return jnp.concatenate([right, x, left], axis=0)


def dot(a, b):
    return jnp.dot(a, b, preferred_element_type=F32)


def adjoint_taps(k_ref, p):
    row = lax.broadcasted_iota(jnp.int32, (C, C), 0)
    col = lax.broadcasted_iota(jnp.int32, (C, C), 1)
    one = jnp.where(row == col, 1.0, 0.0).astype(BF16)
    stacked = jnp.concatenate([k_ref[p, 2], k_ref[p, 1], k_ref[p, 0]], axis=0)
    return lax.dot_general(one, stacked, NT, preferred_element_type=F32).astype(BF16)


def step_kernel(grid, factor, f_any, t_any, k1_any, k2_any, m_any, out_ref, g_ref,
                f_ref, t_ref, k1_ref, k2_ref, m_ref,
                ft, tt, ts, f3, y, z, hid, d, ds, fg, dh, taps, near, far, acc, flat,
                load_sem, halo_send, halo_recv, outer_sem, *net):
    loads = [pltpu.make_async_copy(source, target, load_sem.at[n]) for n, (source, target) in enumerate(
        ((f_any, f_ref), (t_any, t_ref), (k1_any, k1_ref), (k2_any, k2_ref), (m_any, m_ref)))]
    for load in loads:
        load.start()
    dp, lon = lax.axis_index("dp"), lax.axis_index("lon")
    lon_size = lax.axis_size("lon")
    right = (dp, lax.rem(lon + 1, lon_size))
    left = (dp, lax.rem(lon + lon_size - 1, lon_size))
    barrier = pltpu.get_barrier_semaphore()
    greeted = grid.greet(barrier, left, right)

    def turner(source, target):
        def turn(k):
            rows = pl.ds(k * 16, 16)
            target[2:2 + COLS, rows, :] = jnp.swapaxes(source[rows], 0, 1)
        return turn

    copies = []
    for index, (source, ref) in enumerate(((f_ref, ft), (t_ref, tt))):
        loads[index].wait()
        for k in range(C // 16):
            turner(source, ref)(k)
        pair = [send(ref.at[COLS + 1], ref.at[1],
                     halo_send.at[2 * index], halo_recv.at[2 * index], right),
                send(ref.at[2], ref.at[COLS + 2],
                     halo_send.at[2 * index + 1], halo_recv.at[2 * index + 1], left)]
        copies += pair
    pl.semaphore_wait(barrier, greeted)
    for copy in copies:
        copy.start()

    for load in loads[2:]:
        load.wait()
    for p in range(3):
        taps[p * C:(p + 1) * C, :] = jnp.concatenate([k1_ref[p, 0], k1_ref[p, 1], k1_ref[p, 2]], axis=1)
    for index, k_ref in enumerate((k1_ref, k2_ref)):
        far[index] = jnp.concatenate([adjoint_taps(k_ref, 0), adjoint_taps(k_ref, 2)], axis=0)
        near[index] = adjoint_taps(k_ref, 1)
    metric = m_ref[...].reshape(1, LAT)

    def adjoint_block(index, slots, plain, scaled):
        p3 = jnp.concatenate([moved_rows(v) for v in plain], axis=1)
        s3 = jnp.concatenate([moved_rows(v) for v in scaled], axis=1)
        zn = dot(near[index], p3)
        zf = dot(far[index], s3)
        for n, s in enumerate(slots):
            z[s, :2 * C] = zf[:, n * LAT:(n + 1) * LAT]
            z[s, 2 * C:] = zn[:, n * LAT:(n + 1) * LAT]

    def forward_block(slots):
        rows = [moved_rows(ft[s]) for s in slots]
        for n, s in enumerate(slots):
            f3[s] = rows[n]
        yb = dot(taps[...], jnp.concatenate(rows, axis=1))
        for n, s in enumerate(slots):
            y[s] = yb[:, n * LAT:(n + 1) * LAT]

    def reverse_block(slots):
        plain = [tt[s] for s in slots]
        scaled = [(v.astype(F32) * metric).astype(BF16) for v in plain]
        for n, s in enumerate(slots):
            ts[s] = scaled[n]
        adjoint_block(1, slots, plain, scaled)

    def first_block(slots):
        forward_block(slots)
        reverse_block(slots)

    def adjoint_sum(s):
        return z[s, 2 * C:] + z[s - 1, C:2 * C] + z[s + 1, :C]

    def middle(s):
        u = y[s, C:2 * C] + metric * (y[s - 1, :C] + y[s + 1, 2 * C:])
        square = u * u
        inner = jnp.tanh(gelu_coef * (u + 0.044715 * square * u))
        half = 0.5 * (1.0 + inner)
        slope = half + (0.5 * gelu_coef) * u * (1.0 - inner * inner) * (1.0 + 3.0 * 0.044715 * square)
        hid[s] = (u * half).astype(BF16)
        delta = (adjoint_sum(s) * slope).astype(BF16)
        d[s] = delta
        ds[s] = (delta.astype(F32) * metric).astype(BF16)

    def middle_two(s):
        middle(s)
        middle(s + 1)

    def trio(plain, scaled, s):
        return jnp.concatenate([scaled[s + 1], plain[s], scaled[s - 1]], axis=0)

    def second_term(slots):
        h3 = jnp.concatenate([moved_rows(hid[s]) for s in slots], axis=1)
        e3 = jnp.concatenate([trio(tt, ts, s) for s in slots], axis=1)
        acc[1] += lax.dot_general(e3, h3, NT, preferred_element_type=F32)

    def first_term(slots):
        v3 = jnp.concatenate([f3[s] for s in slots], axis=1)
        d3 = jnp.concatenate([trio(d, ds, s) for s in slots], axis=1)
        acc[0] += lax.dot_general(d3, v3, NT, preferred_element_type=F32)

    def terms(b):
        second_term([3 + 7 * b + n for n in range(7)])
        first_term([4 + 6 * b + n for n in range(6)])

    acc[...] = jnp.zeros_like(acc)
    for s in (0, 1, COLS + 2, COLS + 3):
        d[s] = jnp.zeros((C, LAT), BF16)
        ds[s] = jnp.zeros((C, LAT), BF16)
    for b in range(2):
        first_block([2 + 8 * b + n for n in range(8)])
    for b in range(7):
        middle(3 + b)
    second_term([3 + n for n in range(7)])
    for b in range(7, 14):
        middle(3 + b)
    second_term([10 + n for n in range(7)])
    reduction = Reduction(grid, factor, *net)

    def pack(index):
        base = index * GRAD_ROWS
        flat[base:base + 192, :] = acc[index, :, :128]
        flat[base + 192:base + GRAD_ROWS, :] = jnp.concatenate([acc[index, :96, 128:], acc[index, 96:, 128:]], axis=1)
        reduction.pack(flat, index)

    edges = [1, COLS + 2]
    for copy in copies[:2]:
        copy.wait_recv()
    forward_block(edges)
    for copy in copies[2:]:
        copy.wait_recv()
    reverse_block(edges)
    middle(2)
    middle(COLS + 1)
    second_term([2, COLS + 1])
    pack(1)
    reduction.scatter(1)
    first_term([1 + n for n in range(9)])
    first_term([10 + n for n in range(9)])
    pack(0)
    reduction.scatter(0)
    reduction.scatter_partner()
    outer = [send(d.at[COLS + 1], dh.at[0], outer_sem.at[0], outer_sem.at[2], right),
             send(d.at[2], dh.at[1], outer_sem.at[1], outer_sem.at[3], left)]
    for copy in outer:
        copy.start()

    def last_block(slots):
        adjoint_block(0, slots, [d[s] for s in slots], [ds[s] for s in slots])

    def finish(s):
        fg[s - 2] = (tt[s].astype(F32) + adjoint_sum(s)).astype(BF16)

    def finish_two(b):
        finish(3 + 2 * b)
        finish(4 + 2 * b)

    def turn_back(k):
        part = pl.ds(pl.multiple_of(k * 16, 16), 16)
        out_ref[part] = jnp.swapaxes(fg[:, part, :], 0, 1)

    loop(0, 4, lambda b: last_block([2 + 4 * b + n for n in range(4)]))
    loop(0, COLS // 2 - 1, finish_two)
    reduction.after_plane()
    for copy in copies:
        copy.wait_send()
    for n, s in enumerate(edges):
        outer[n].wait_recv()
        d[s] = dh[n]
        ds[s] = (dh[n].astype(F32) * metric).astype(BF16)
    last_block(edges)
    finish(2)
    finish(COLS + 1)
    loop(0, C // 16, turn_back)
    reduction.after_deep()
    for copy in outer:
        copy.wait_send()
    reduction.drain()
    reduction.finish()
    g_ref[...] = reduction.whole[...]


def format_kernel(grid, x_ref, g_ref, out_ref, g1_ref, g2_ref, flat, sem):
    copy = pltpu.make_async_copy(x_ref, out_ref, sem)
    copy.start()
    rows = grid.rows
    for g in range(TOTAL_ROWS // rows):
        flat[g * rows:(g + 1) * rows, :] = g_ref[g].astype(F32)
    for index, ref in enumerate((g1_ref, g2_ref)):
        for p in range(3):
            base = index * GRAD_ROWS + p * C
            pair = flat[base:base + C, :]
            ref[p, 0] = pair[:, :C].astype(BF16)
            ref[p, 1] = pair[:, C:].astype(BF16)
        side = flat[index * GRAD_ROWS + 192:(index + 1) * GRAD_ROWS, :]
        rest = jnp.concatenate([side[:, :C], side[:, C:]], axis=0)
        for p in range(3):
            ref[p, 2] = rest[p * C:(p + 1) * C].astype(BF16)
    copy.wait()


def per_device(fields, cotangent, kernel_first, kernel_second, metric):
    dp_size, lon_size = lax.axis_size("dp"), lax.axis_size("lon")
    grid = Grid(dp_size, lon_size)
    factor = 1.0 / (float(dp_size) * float(COLS * lon_size) * float(LAT)) ** 0.5
    vmem = pl.BlockSpec(memory_space=pltpu.VMEM)
    anywhere = pl.BlockSpec(memory_space=pl.ANY)
    taps = (3, 3, C, C)
    column = pltpu.VMEM((SLOTS, C, LAT), BF16)
    turned, packed = pl.pallas_call(
        functools.partial(step_kernel, grid, factor),
        out_shape=(
            pltpu.VMEM((C, COLS, LAT), BF16),
            pltpu.VMEM((grid.plane, grid.rows, 128), BF16),
        ),
        in_specs=[anywhere] * 5,
        out_specs=(vmem, vmem),
        scratch_shapes=[
            pltpu.VMEM((C, COLS, LAT), BF16),
            pltpu.VMEM((C, COLS, LAT), BF16),
            pltpu.VMEM(taps, BF16),
            pltpu.VMEM(taps, BF16),
            pltpu.VMEM((LAT,), F32),
            column,
            column,
            column,
            pltpu.VMEM((SLOTS, 3 * C, LAT), BF16),
            pltpu.VMEM((SLOTS, 3 * C, LAT), F32),
            pltpu.VMEM((SLOTS, 3 * C, LAT), F32),
            column,
            column,
            column,
            pltpu.VMEM((COLS, C, LAT), BF16),
            pltpu.VMEM((2, C, LAT), BF16),
            pltpu.VMEM((3 * C, 3 * C), BF16),
            pltpu.VMEM((2, C, 3 * C), BF16),
            pltpu.VMEM((2, 2 * C, 3 * C), BF16),
            pltpu.VMEM((2, 3 * C, 3 * C), F32),
            pltpu.VMEM((TOTAL_ROWS, 128), F32),
            pltpu.SemaphoreType.DMA((5,)),
            pltpu.SemaphoreType.DMA((4,)),
            pltpu.SemaphoreType.DMA((4,)),
            pltpu.SemaphoreType.DMA((4,)),
        ] + net_scratch(grid),
        compiler_params=pltpu.CompilerParams(
            collective_id=0, has_side_effects=True, vmem_limit_bytes=60 * 2**20),
    )(fields[0], cotangent[0], kernel_first, kernel_second, metric)
    field_grad, first, second = pl.pallas_call(
        functools.partial(format_kernel, grid),
        out_shape=(
            jax.ShapeDtypeStruct((C, COLS, LAT), BF16),
            jax.ShapeDtypeStruct(taps, BF16),
            jax.ShapeDtypeStruct(taps, BF16),
        ),
        in_specs=[vmem, vmem],
        out_specs=(anywhere, vmem, vmem),
        scratch_shapes=[pltpu.VMEM((TOTAL_ROWS, 128), F32), pltpu.SemaphoreType.DMA(())],
        compiler_params=pltpu.CompilerParams(vmem_limit_bytes=16 * 2**20),
    )(turned, packed)
    return field_grad[None], first, second


def solution(mesh):
    placed = (P("dp", None, "lon", None), P("dp", None, "lon", None), P(), P(), P())
    return jax.shard_map(
        per_device,
        mesh=mesh,
        in_specs=placed,
        out_specs=(P("dp", None, "lon", None), P(), P()),
        check_vma=False,
    )
```
